32 devices in a mesh: dp: 8 (over y, x, core), tensor: 4 (over z).
Axes of the slice: x: 2, y: 2, z: 4, core: 2. Of those that a mesh axis runs over, the one named last changes fastest.
Arguments:
- block_input: bfloat16 [4096, 1024], P(('dp', 'tensor')), may hold values from -6 to 6
- segment_ids: int32 [8, 512], P('dp'), may hold values from 0 to 3, never falling along the last dimension, each value on 1 to 256 neighbouring positions
- attention_norm_gain: float32 [1024], replicated, may hold values from 0.1 to 1.9
- w_qkv: bfloat16 [1024, 2048], P('dp', 'tensor'), may hold values from -0.1875 to 0.1875
- w_og: bfloat16 [1024, 1024], P('dp', 'tensor'), may hold values from -0.1875 to 0.1875
- w_beta: bfloat16 [1024, 4], P('dp', 'tensor'), may hold values from -0.1875 to 0.1875
- w_alpha: bfloat16 [1024, 4], P('dp', 'tensor'), may hold values from -0.1875 to 0.1875
- conv_weight: float32 [4, 2048], P(None, 'tensor'), may hold values from -3 to 3
- a_log: float32 [4], P('tensor'), may hold values from -6 to -1
- dt_bias: float32 [4], P('tensor'), may hold values from -2 to 1
- out_gain: float32 [256], replicated, may hold values from 0.1 to 1.9
- w_out: bfloat16 [1024, 1024], P('tensor', 'dp'), may hold values from -0.1875 to 0.1875
- ffn_gain: float32 [1024], replicated, may hold values from 0.1 to 1.9
- w_ffn_gate: bfloat16 [1024, 2816], P('dp', 'tensor'), may hold values from -0.1875 to 0.1875
- w_ffn_up: bfloat16 [1024, 2816], P('dp', 'tensor'), may hold values from -0.1875 to 0.1875
- w_ffn_down: bfloat16 [2816, 1024], P('tensor', 'dp'), may hold values from -0.109375 to 0.109375
- cotangent: bfloat16 [4096, 1024], P(('dp', 'tensor')), may hold values from -6 to 6
Outputs:
- block_output: bfloat16 [4096, 1024], P(('dp', 'tensor'))
- input_grad: float32 [4096, 1024], P(('dp', 'tensor'))
- attn_gain_grad: float32 [1024], replicated
- w_qkv_grad: float32 [1024, 2048], P('dp', 'tensor')
- w_og_grad: float32 [1024, 1024], P('dp', 'tensor')
- w_beta_grad: float32 [1024, 4], P('dp', 'tensor')
- w_alpha_grad: float32 [1024, 4], P('dp', 'tensor')
- conv_weight_grad: float32 [4, 2048], P(None, 'tensor')
- a_log_grad: float32 [4], P('tensor')
- dt_bias_grad: float32 [4], P('tensor')
- out_gain_grad: float32 [256], replicated
- w_out_grad: float32 [1024, 1024], P('tensor', 'dp')
- ffn_gain_grad: float32 [1024], replicated
- w_ffn_gate_grad: float32 [1024, 2816], P('dp', 'tensor')
- w_ffn_up_grad: float32 [1024, 2816], P('dp', 'tensor')
- w_ffn_down_grad: float32 [2816, 1024], P('tensor', 'dp')
The draws below stay inside these ranges and needn't reach their ends.
Inputs may be any that keep to these rules, and one draw needn't show every extreme that they name: `segment_ids`: along each sequence the document ids never fall; each of the 4 documents covers 1 to 256 positions, and some document has exactly 256.
All inputs are finite; a program needn't handle non-finite values.
Results may differ from the reference program's by a relative error of at most 0.012.
Values may be sent and summed in bfloat16 or wider, within the bound.
A program may use at most 128 MiB of HBM per device.

```python
import math
from functools import partial
import jax
import jax.numpy as jnp
import numpy as np
from jax import lax

D = 1024
H = 4
DK = 128
DV = 256
FF = 2816
KC = 4
LEN = 512
DOCS = 4
DOC_MOST = 256
CONV = 2048
HV = 1024
NSEQ = 8
TOKENS = 4096


def steps_of(own_key, shape, pieces, low, high):
    gain = 1.0
    for position, shards_of in pieces:
        heights = jax.random.uniform(jax.random.fold_in(jax.random.fold_in(own_key, 6), position), (shards_of,), jnp.float32, low / len(pieces), high / len(pieces))
        gain = gain * jnp.repeat(jnp.exp(heights), shape[position] // shards_of).reshape((-1,) + (1,) * (len(shape) - 1 - position))
    return gain


def split_up(number_of, total, bound, lean):
    loads = [(1 << 20) // math.isqrt(grade ** lean) + 1 for grade in range(2, number_of + 1)]
    spare, counts = total - bound - (number_of - 1), [1] * (number_of - 1)
    while spare > 0:
        candidates = [i for i in range(number_of - 1) if counts[i] < bound]
        pool, remaining = sum([loads[i] for i in candidates]), spare
        for i in candidates:
            more = min(bound - counts[i], max(1, remaining * loads[i] // pool), spare)
            counts[i] = counts[i] + more
            spare = spare - more
    return np.array([bound] + counts)


def uneven(key, count, total, most, lean):
    if count == 2:
        one = jax.random.randint(key, (), max(1, total - most), min(most, total - 1) + 1)
        return jnp.stack([one, total - one])
    lengths = jnp.asarray(split_up(count, total, most, lean), jnp.int32)
    pairs = (count - 1) // 2
    donor, taker = lengths[1:1 + 2 * pairs:2], lengths[2:2 + 2 * pairs:2]
    margin = jnp.minimum(donor - 1, most - taker)
    moved = jax.random.randint(jax.random.fold_in(key, 1), (pairs,), 0, 1 << 20) % (margin + 1)
    lengths = lengths.at[1:1 + 2 * pairs:2].set(donor - moved).at[2:2 + 2 * pairs:2].set(taker + moved)
    return lengths[jax.random.permutation(jax.random.fold_in(key, 2), count)]


def gaussian(rng, dims, scale, most, shards=(), kind=jnp.bfloat16):
    values = scale * jax.random.normal(rng, dims, jnp.float32)
    if shards:
        values = values * steps_of(rng, dims, shards, -0.22, 0.18)
    return jnp.clip(values, -most, most).astype(kind)


def setup_inputs(seed: int = 0) -> dict:
    key_list = jax.random.split(jax.random.key(seed), 18)
    return {
        "block_input": gaussian(key_list[0], (TOKENS, D), 1.0, 6.0, ((0, 32),)),
        "segment_ids": jax.vmap(lambda own: jnp.searchsorted(jnp.cumsum(uneven(own, DOCS, LEN, DOC_MOST, 0)), jnp.arange(LEN), side="right"))(jax.random.split(key_list[1], NSEQ)).reshape((NSEQ, LEN)).astype(jnp.int32),
        "attention_norm_gain": jnp.clip(1.0 + 0.18 * jax.random.normal(key_list[2], (D,), jnp.float32), 0.1, 1.9),
        "w_qkv": gaussian(key_list[3], (D, CONV), D ** -0.5, 0.1875, ((0, 8), (1, 4))),
        "w_og": gaussian(key_list[4], (D, HV), D ** -0.5, 0.1875, ((0, 8), (1, 4))),
        "w_beta": gaussian(key_list[5], (D, H), D ** -0.5, 0.1875, ((0, 8), (1, 4))),
        "w_alpha": gaussian(key_list[6], (D, H), D ** -0.5, 0.1875, ((0, 8), (1, 4))),
        "conv_weight": gaussian(key_list[7], (KC, CONV), KC ** -0.5, 3.0, ((1, 4),), jnp.float32),
        "a_log": jnp.clip(-6.0 + 5.0 * jax.random.uniform(key_list[8], (H,), jnp.float32) ** steps_of(key_list[8], (H,), ((0, 4),), -0.2, 0.2), -6.0, -1.0),
        "dt_bias": jnp.clip(-2.0 + 3.0 * jax.random.uniform(key_list[9], (H,), jnp.float32) ** steps_of(key_list[9], (H,), ((0, 4),), -0.2, 0.2), -2.0, 1.0),
        "out_gain": jnp.clip(1.0 + 0.18 * jax.random.normal(key_list[10], (DV,), jnp.float32), 0.1, 1.9),
        "w_out": gaussian(key_list[11], (HV, D), HV ** -0.5, 0.1875, ((0, 4), (1, 8))),
        "ffn_gain": jnp.clip(1.0 + 0.18 * jax.random.normal(key_list[12], (D,), jnp.float32), 0.1, 1.9),
        "w_ffn_gate": gaussian(key_list[13], (D, FF), D ** -0.5, 0.1875, ((0, 8), (1, 4))),
        "w_ffn_up": gaussian(key_list[14], (D, FF), D ** -0.5, 0.1875, ((0, 8), (1, 4))),
        "w_ffn_down": gaussian(key_list[15], (FF, D), FF ** -0.5, 0.109375, ((0, 4), (1, 8))),
        "cotangent": gaussian(key_list[16], (TOKENS, D), 1.0, 6.0, ((0, 32),)),
    }


HIGHEST = lax.Precision.HIGHEST

def matmul(left, right):
    return jnp.dot(left, right, preferred_element_type=jnp.float32)

def contract(form, left, right):
    return jnp.einsum(form, left, right, precision=HIGHEST)

def short_conv(mixer_in, conv_weight, segment):
    taps = conv_weight.shape[0]
    total = conv_weight[taps - 1] * mixer_in
    for offset in range(1, taps):
        shifted = jnp.concatenate([jnp.zeros((offset, mixer_in.shape[1]), mixer_in.dtype), mixer_in[:-offset]], 0)
        earlier = jnp.concatenate([jnp.full((offset,), -1, jnp.int32), segment[:-offset]], 0)
        same_doc = (earlier == segment).astype(mixer_in.dtype)
        total = total + conv_weight[taps - 1 - offset] * shifted * same_doc[:, None]
    return jax.nn.silu(total)

def split_heads(activated, heads):
    grouped = activated.reshape(activated.shape[0], heads, 2 * DK + DV)
    query = grouped[..., :DK]
    keys = grouped[..., DK:2 * DK]
    values = grouped[..., 2 * DK:]
    query = query * lax.rsqrt(lax.optimization_barrier(jnp.sum(query * query, -1, keepdims=True)) + 1e-06) * DK ** (-0.5)
    keys = keys * lax.rsqrt(lax.optimization_barrier(jnp.sum(keys * keys, -1, keepdims=True)) + 1e-06)
    return (query, keys, values)

def gated_norm(output_heads, gate_in, out_gain):
    rows, heads = (output_heads.shape[0], output_heads.shape[1])
    gate_heads = gate_in.reshape(rows, heads, DV)
    normed = output_heads * lax.rsqrt(lax.optimization_barrier(jnp.mean(output_heads * output_heads, -1, keepdims=True)) + 1e-05) * out_gain
    return (normed * jax.nn.silu(gate_heads)).reshape(rows, heads * DV)

def mixer_core(segment, mixer_in, gate_in, beta_in, decay_in, conv_weight, a_log, dt_bias, out_gain):
    heads = a_log.shape[0]
    query, keys, values = split_heads(short_conv(mixer_in, conv_weight, segment), heads)
    strength = jax.nn.sigmoid(beta_in)
    log_decay = -jnp.exp(a_log) * jax.nn.softplus(decay_in + dt_bias)
    earlier = jnp.concatenate([jnp.full((1,), -1, jnp.int32), segment[:-1]], 0)
    factor = jnp.exp(log_decay) * (earlier == segment).astype(log_decay.dtype)[:, None]

    def advance(state, inputs):
        query_now, key_now, value_now, strength_now, factor_now = inputs
        decayed = factor_now[:, None, None] * state
        predicted = contract('hvk,hk->hv', decayed, key_now)
        update = strength_now[:, None] * (value_now - predicted)
        state = decayed + update[:, :, None] * key_now[:, None, :]
        return (state, contract('hvk,hk->hv', state, query_now))
    initial = jnp.zeros((heads, DV, DK), mixer_in.dtype)
    _, output_heads = lax.scan(advance, initial, (query, keys, values, strength, factor))
    return gated_norm(output_heads, gate_in, out_gain)

def root_mean_square_forward(rows):
    inverse_scale = lax.rsqrt(lax.optimization_barrier(jnp.mean(rows * rows, -1, keepdims=True)) + 1e-06)
    return (rows * inverse_scale, inverse_scale)

def root_mean_square_backward(normalized_input, inverse_scale, norm_gain, upstream_gradient):
    scaled_rows = upstream_gradient * norm_gain
    return (inverse_scale * (scaled_rows - normalized_input * lax.optimization_barrier(jnp.mean(scaled_rows * normalized_input, -1, keepdims=True))), lax.optimization_barrier(jnp.sum(upstream_gradient * normalized_input, 0)))

def reference(block_input, segment_ids, attention_norm_gain, w_qkv, w_og, w_beta, w_alpha, conv_weight, a_log, dt_bias, out_gain, w_out, ffn_gain, w_ffn_gate, w_ffn_up, w_ffn_down, cotangent):
    shapes = [attention_norm_gain, w_qkv, w_og, w_beta, w_alpha, conv_weight, a_log, dt_bias, out_gain, w_out, ffn_gain, w_ffn_gate, w_ffn_up, w_ffn_down]
    zero_grads = tuple((jnp.zeros(item.shape, jnp.float32) for item in shapes))

    def one_sequence(totals, inputs):
        input_seq, segment, grad_seq = inputs
        residual_input = input_seq.astype(jnp.float32)
        attention_normalized_input, attention_scale = root_mean_square_forward(residual_input)
        attention_normed = (attention_normalized_input * attention_norm_gain).astype(jnp.bfloat16)
        mixer_in = matmul(attention_normed, w_qkv)
        gate_in = matmul(attention_normed, w_og)
        beta_in = matmul(attention_normed, w_beta)
        decay_in = matmul(attention_normed, w_alpha)
        mixed_full, core_back = jax.vjp(partial(mixer_core, segment), mixer_in, gate_in, beta_in, decay_in, conv_weight, a_log, dt_bias, out_gain)
        mixed = mixed_full.astype(jnp.bfloat16)
        resid_mid = residual_input + matmul(mixed, w_out)
        hhat, scale_ffn = root_mean_square_forward(resid_mid)
        normed_ffn = (hhat * ffn_gain).astype(jnp.bfloat16)
        fgate = matmul(normed_ffn, w_ffn_gate)
        fup = matmul(normed_ffn, w_ffn_up)
        sigma = jax.nn.sigmoid(fgate)
        hidden = (fgate * sigma * fup).astype(jnp.bfloat16)
        out_seq = (resid_mid + matmul(hidden, w_ffn_down)).astype(jnp.bfloat16)
        dhidden = matmul(grad_seq, w_ffn_down.T)
        dfgate = (dhidden * fup * sigma * (1.0 + fgate * (1.0 - sigma))).astype(jnp.bfloat16)
        dfup = (dhidden * fgate * sigma).astype(jnp.bfloat16)
        grad_down = matmul(hidden.T, grad_seq)
        grad_fgate = matmul(normed_ffn.T, dfgate)
        grad_fup = matmul(normed_ffn.T, dfup)
        dnormed_ffn = matmul(dfgate, w_ffn_gate.T) + matmul(dfup, w_ffn_up.T)
        dresid_norm, grad_ffn_gain = root_mean_square_backward(hhat, scale_ffn, ffn_gain, dnormed_ffn)
        dresid = grad_seq.astype(jnp.float32) + dresid_norm
        dresid_b = dresid.astype(jnp.bfloat16)
        grad_out = matmul(mixed.T, dresid_b)
        dmixed = matmul(dresid_b, w_out.T)
        dmixer_f, dgate_f, dbeta_f, ddecay_f, grad_conv, grad_alog, grad_dt, grad_ogain = core_back(dmixed)
        dmixer_b = dmixer_f.astype(jnp.bfloat16)
        dgate_b = dgate_f.astype(jnp.bfloat16)
        dbeta_b = dbeta_f.astype(jnp.bfloat16)
        ddecay_b = ddecay_f.astype(jnp.bfloat16)
        grad_qkv = matmul(attention_normed.T, dmixer_b)
        grad_og = matmul(attention_normed.T, dgate_b)
        grad_beta = matmul(attention_normed.T, dbeta_b)
        grad_alpha = matmul(attention_normed.T, ddecay_b)
        attention_normed_gradient = matmul(dmixer_b, w_qkv.T) + matmul(dgate_b, w_og.T) + matmul(dbeta_b, w_beta.T) + matmul(ddecay_b, w_alpha.T)
        norm_input_gradient, attention_gain_gradient = root_mean_square_backward(attention_normalized_input, attention_scale, attention_norm_gain, attention_normed_gradient)
        input_grad_seq = dresid + norm_input_gradient
        new_grads = (attention_gain_gradient, grad_qkv, grad_og, grad_beta, grad_alpha, grad_conv, grad_alog, grad_dt, grad_ogain, grad_out, grad_ffn_gain, grad_fgate, grad_fup, grad_down)
        totals = jax.tree.map(lambda left, right: left + right.astype(left.dtype), totals, new_grads)
        return (totals, (out_seq, input_grad_seq))
    input_seqs = block_input.reshape(NSEQ, LEN, D)
    grad_seqs = cotangent.reshape(NSEQ, LEN, D)
    totals, (out_all, input_grad_all) = lax.scan(one_sequence, zero_grads, (input_seqs, segment_ids, grad_seqs))
    return (out_all.reshape(TOKENS, D), input_grad_all.reshape(TOKENS, D), totals[0], totals[1], totals[2], totals[3], totals[4], totals[5], totals[6], totals[7], totals[8], totals[9], totals[10], totals[11], totals[12], totals[13])
```

```python
import functools

import jax
import jax.numpy as jnp
from jax import lax
from jax.experimental import pallas as pl
from jax.experimental.pallas import tpu as pltpu
from jax.sharding import PartitionSpec as P

DK = 128
DV = 256
BLOCK = 128
PAD = 8
LANES = 128
F32 = jnp.float32
BF16 = jnp.bfloat16
HIGHEST = lax.Precision.HIGHEST
MESH = pl.DeviceIdType.MESH


def contract(left, right, left_dim, right_dim):
    return lax.dot_general(
        left, right, (((left_dim,), (right_dim,)), ((), ())), preferred_element_type=F32
    )


def nn(left, right):
    return contract(left, right, 1, 0)


def nt(left, right):
    return contract(left, right, 1, 1)


def dot(left, right, left_dim, right_dim):
    return lax.dot_general(
        left,
        right,
        (((left_dim,), (right_dim,)), ((), ())),
        precision=HIGHEST,
        preferred_element_type=F32,
    )


def grid_index():
    row = lax.broadcasted_iota(jnp.int32, (BLOCK, BLOCK), 0)
    column = lax.broadcasted_iota(jnp.int32, (BLOCK, BLOCK), 1)
    return row, column


def to_row(column_vector):
    row, column = grid_index()
    return jnp.sum(jnp.where(row == column, column_vector, 0.0), 0, keepdims=True)


def to_column(row_vector):
    row, column = grid_index()
    return jnp.sum(jnp.where(row == column, row_vector, 0.0), 1, keepdims=True)


def unit_lower_inverses(lowers):
    row, column = grid_index()
    span = 1
    results = None
    while span < BLOCK:
        pair = (row // (2 * span) == column // (2 * span)) & (row // span != column // span)
        corners = [jnp.where(pair, lower, 0.0) for lower in lowers]
        if results is None:
            identity = (row == column).astype(F32)
            results = [identity - corner for corner in corners]
        else:
            halves = [dot(corner, result, 1, 0) for corner, result in zip(corners, results)]
            results = [result - dot(result, half, 1, 0) for result, half in zip(results, halves)]
        span = span * 2
    return results


def inverse_rms(rows, epsilon):
    return lax.rsqrt(jnp.mean(rows * rows, -1, keepdims=True) + epsilon)


def softplus(value):
    return jnp.maximum(value, 0.0) + jnp.log1p(jnp.exp(-jnp.abs(value)))


class Refs:
    def __init__(self, names, refs):
        for name, ref in zip(names, refs):
            setattr(self, name, ref)


Z_X, Z_COT, Z_WOUT, Z_DN2, Z_DRES, Z_Y, Z_DN1, Z_SMALL, Z_MIXED = range(9)


def kernel(cfg, names, *refs):
    r = Refs(names, refs)
    T, N, S, R, L, D = cfg["T"], cfg["N"], cfg["S"], cfg["R"], cfg["L"], cfg["D"]
    NI, F, c0, c1 = cfg["NI"], cfg["F"], cfg["c0"], cfg["c1"]
    bits = N.bit_length() - 1
    blocks = L // BLOCK
    me_z = lax.axis_index("tensor")
    me_d = lax.axis_index("dp")
    sends = []

    def bit(b):
        return lax.rem(lax.div(me_d, 1 << b), 2)

    def flipped(which):
        place = me_d
        for b in which:
            place = place + (1 << b) * (1 - 2 * bit(b))
        return place

    barrier = pltpu.get_barrier_semaphore()
    for p in range(T):

        @pl.when(p != me_z)
        def _():
            pl.semaphore_signal(barrier, inc=1, device_id={"tensor": p}, device_id_type=MESH)

    for b in range(bits):
        pl.semaphore_signal(barrier, inc=1, device_id={"dp": flipped([b])}, device_id_type=MESH)
    pl.semaphore_wait(barrier, T - 1 + bits)

    def z_copy(k, p, src, dst, source):
        return pltpu.make_async_remote_copy(
            src_ref=src,
            dst_ref=dst,
            send_sem=r.z_send.at[k, p],
            recv_sem=r.z_recv.at[k, source],
            device_id={"tensor": p},
            device_id_type=MESH,
        )

    def z_start(k, src, dst, peers=None):
        for p in range(T) if peers is None else peers:

            @pl.when(p != me_z)
            def _():
                z_copy(k, p, src(p), dst, me_z).start()

            sends.append((k, p, src))

    def z_wait(k, landing, peers=None, then=None):
        for p in range(T) if peers is None else peers:

            @pl.when(p != me_z)
            def _():
                z_copy(k, p, landing(p), landing(p), p).wait_recv()
                if then is not None:
                    then(p)

    class Gather:
        def __init__(self, index, own, place, order):
            self.index, self.own, self.place, self.order = index, own, place, order

        def copies(self, s, arriving):
            out = []
            for subset in range(1 << s):
                which = [self.order[t] for t in range(s) if subset >> t & 1]
                j = flipped(which + ([self.order[s]] if arriving else []))
                src = self.own if not which and not arriving else self.place(j)
                n = (1 << s) - 1 + subset
                out.append(
                    pltpu.make_async_remote_copy(
                        src_ref=src,
                        dst_ref=self.place(j),
                        send_sem=r.g_send.at[self.index, n],
                        recv_sem=r.g_recv.at[self.index, n],
                        device_id={"dp": flipped([self.order[s]])},
                        device_id_type=MESH,
                    )
                )
            return out

        def start(self, s):
            if s < bits:
                for copy in self.copies(s, False):
                    copy.start()

        def wait(self, s):
            if s < bits:
                for copy in self.copies(s, True):
                    copy.wait_recv()

        def step(self, s):
            self.wait(s)
            self.start(s + 1)

        def finish(self, s):
            for t in range(s, bits):
                self.step(t)

        def drain(self):
            for s in range(bits):
                for copy in self.copies(s, False):
                    copy.wait_send()

    upward = list(range(1, bits)) + [0]
    downward = list(reversed(range(1, bits))) + [0]

    def shard_of(ref):
        return lambda j: ref.at[pl.ds(pl.multiple_of(j * S, S), S), :]

    def shard_of3(ref):
        return lambda j: ref.at[:, pl.ds(pl.multiple_of(j * S, S), S), :]

    own_rows = pl.ds(pl.multiple_of(me_d * S, S), S)
    g_in = Gather(0, r.w_in, shard_of(r.w_in_all), upward)
    g_gu = Gather(1, r.w_gu, shard_of(r.w_gu_all), upward)
    g_d = Gather(2, r.w_d, shard_of(r.w_d_all), downward)
    g_out = Gather(3, shard_of3(r.w_out_all)(me_d), shard_of3(r.w_out_all), downward)

    class Reduce:
        def __init__(self, index, keep, send, recv, out, order):
            self.index, self.keep, self.send, self.recv, self.out = index, keep, send, recv, out
            self.order = order

        def copy(self, level):
            return pltpu.make_async_remote_copy(
                src_ref=self.send[level],
                dst_ref=self.recv[level],
                send_sem=r.r_send.at[self.index, level],
                recv_sem=r.r_recv.at[self.index, level],
                device_id={"dp": flipped([self.order[level]])},
                device_id_type=MESH,
            )

        def start(self, level):
            self.copy(level).start()

        def step(self, level):
            self.copy(level).wait_recv()
            keep, recv = self.keep, self.recv[level]

            def part(j):
                rows = pl.ds(pl.multiple_of(j * S, S), S)
                return keep[rows, :] + recv[rows, :].astype(F32)

            if level + 1 == bits:
                self.out[...] = part(0)
                return
            half = N >> (level + 2)
            mine = bit(self.order[level + 1])
            low_first = self.order is reduce_up

            def body(q, carry):
                if low_first:
                    a, b = 2 * q + mine, 2 * q + 1 - mine
                else:
                    a, b = q + half * mine, q + half * (1 - mine)
                stay, leave = part(a), part(b)
                rows = pl.ds(pl.multiple_of(q * S, S), S)
                keep[rows, :] = stay
                self.send[level + 1][rows, :] = leave.astype(BF16)
                return carry

            lax.fori_loop(0, half, body, 0)
            self.start(level + 1)

        def drain(self):
            for level in range(bits):
                self.copy(level).wait_send()

    reduce_up = [0] + list(range(1, bits))
    reduce_down = [0] + list(reversed(range(1, bits)))

    def levels(prefix):
        return [getattr(r, prefix + str(level)) for level in range(bits)]

    s_in = Reduce(0, r.k_in, levels("s_in"), levels("v_in"), r.o_in, reduce_up)
    s_gu = Reduce(1, r.k_gu, levels("s_gu"), levels("v_gu"), r.o_gu, reduce_up)
    s_d = Reduce(2, r.k_d, levels("s_d"), levels("v_d"), r.o_d, reduce_down)
    s_out = Reduce(3, r.k_out, levels("s_out"), levels("v_out"), r.o_out, reduce_down)

    def transpose_into(source):
        for i in range(blocks):
            here = slice(i * BLOCK, (i + 1) * BLOCK)
            r.turned[:, here] = source[here, :].T

    def weight_grad(right, columns, sum_of, at):
        wide = columns.stop - columns.start

        def body(p, carry):
            pair = pl.ds(pl.multiple_of(p * 2 * S, 2 * S), 2 * S)
            rows = pl.ds(pl.multiple_of(p * S, S), S)
            r.pair[:, :wide] = nn(r.turned[pair, :], right[:, columns])
            mine, other = bit(0) * S, (1 - bit(0)) * S
            sum_of.keep[rows, at : at + wide] = r.pair[pl.ds(pl.multiple_of(mine, S), S), :wide]
            sum_of.send[0][rows, at : at + wide] = r.pair[
                pl.ds(pl.multiple_of(other, S), S), :wide
            ].astype(BF16)
            return carry

        lax.fori_loop(0, N // 2, body, 0)

    def block_rows(p):
        return pl.ds(p * R if isinstance(p, int) else pl.multiple_of(p * R, R), R)

    own = block_rows(me_z)
    r.x_all[own, :] = r.x[...]
    z_start(Z_X, lambda p: r.x, r.x_all.at[own, :])
    g_in.start(0)
    out_own = r.w_out_all.at[me_z, own_rows, :]
    r.w_out_all[me_z, own_rows, :] = r.w_out[...]
    r.w_in_all[own_rows, :] = r.w_in[...]
    r.w_gu_all[own_rows, :] = r.w_gu[...]
    r.w_d_all[own_rows, :] = r.w_d[...]
    r.cot_all[own, :] = r.cot[...]

    def first_norm(rows):
        x = r.x_all[rows, :].astype(F32)
        r.n1[rows, :] = (x * inverse_rms(x, 1e-06) * r.gain1[...]).astype(BF16)

    first_norm(own)
    g_in.step(0)
    g_d.start(0)
    segment = r.seg[...].astype(F32)
    r.segc[0:PAD, :] = jnp.full((PAD, 1), -1.0, F32)
    r.segc[PAD + L :, :] = jnp.full((PAD, 1), -2.0, F32)
    for i in range(blocks):
        r.segc[PAD + i * BLOCK : PAD + (i + 1) * BLOCK, :] = to_column(
            segment[:, i * BLOCK : (i + 1) * BLOCK]
        )
    r.proj[0:PAD, :] = jnp.zeros((PAD, NI), F32)
    r.dtot[L:, :] = jnp.zeros((PAD, c0), F32)
    g_in.step(1)
    g_gu.start(0)
    z_wait(Z_X, lambda p: r.x_all.at[block_rows(p), :], then=lambda p: first_norm(block_rows(p)))
    z_start(Z_WOUT, lambda p: out_own, out_own)
    z_start(Z_COT, lambda p: r.cot, r.cot_all.at[own, :])
    g_in.finish(2)
    chunk = 2 * R
    chunks = [slice(i * chunk, (i + 1) * chunk) for i in range(L // chunk)]
    for c in chunks:
        r.proj[PAD + c.start : PAD + c.stop, :] = nn(r.n1[c, :], r.w_in_all[...])
    z_wait(Z_WOUT, lambda p: r.w_out_all.at[p, own_rows, :])
    g_out.start(0)
    g_d.step(0)
    g_gu.step(0)

    row, column = grid_index()
    inclusive = row >= column

    def shifted_segment(i, o):
        return r.segc[PAD + i * BLOCK + o : PAD + (i + 1) * BLOCK + o, :]

    def conv_total(i):
        base = PAD + i * BLOCK
        now = shifted_segment(i, 0)
        total = r.conv_w[3:4, :] * r.proj[base : base + BLOCK, :c0]
        for o in range(1, 4):
            same = (shifted_segment(i, -o) == now).astype(F32)
            total = total + r.conv_w[3 - o : 4 - o, :] * (
                r.proj[base - o : base - o + BLOCK, :c0] * same
            )
        return total

    def decays(i):
        base = PAD + i * BLOCK
        both = r.proj[base : base + BLOCK, c1:]
        beta = jax.nn.sigmoid(both[:, 0:1])
        before = both[:, 1:2] + r.dt_bias[...]
        log_decay = -jnp.exp(r.a_log[...]) * softplus(before)
        cum_row = jnp.sum(jnp.where(row <= column, log_decay, 0.0), 0, keepdims=True)
        cum = to_column(cum_row)
        seg_col = shifted_segment(i, 0)
        seg_row = segment[:, i * BLOCK : (i + 1) * BLOCK]
        keep = (seg_col == seg_row) & inclusive
        ratio = jnp.where(keep, jnp.exp(jnp.where(keep, cum - cum_row, 0.0)), 0.0)
        first = PAD + i * BLOCK
        carry = jnp.where(seg_col == r.segc[first - 1 : first, :], jnp.exp(cum), 0.0)
        ends = to_column(ratio[BLOCK - 1 : BLOCK, :])
        last = carry[BLOCK - 1 : BLOCK, :]
        return beta, before, log_decay, ratio, carry, ends, last

    def rows_of(i):
        return slice(i * BLOCK, (i + 1) * BLOCK)

    lowers = []
    for i in range(blocks):
        here = rows_of(i)
        total = conv_total(i)
        active = total * jax.nn.sigmoid(total)
        q, k, v = active[:, :DK], active[:, DK : 2 * DK], active[:, 2 * DK :]
        q = q * lax.rsqrt(jnp.sum(q * q, -1, keepdims=True) + 1e-06) * DK ** (-0.5)
        k = k * lax.rsqrt(jnp.sum(k * k, -1, keepdims=True) + 1e-06)
        r.q[here, :], r.k[here, :], r.v[here, :] = q, k, v
        beta, _, _, ratio, carry, ends, last = decays(i)
        r.ratio[here, :] = ratio
        lowers.append(jnp.where(row > column, beta * ratio * dot(k, k, 1, 1), 0.0))
    g_d.step(1)
    g_gu.step(1)
    inverse_list = unit_lower_inverses(lowers)
    for i in range(blocks):
        r.inverses[rows_of(i), :] = inverse_list[i]
    g_out.step(0)
    state = jnp.zeros((DV, DK), F32)
    for i in range(blocks):
        here = rows_of(i)
        r.states[i * DV : (i + 1) * DV, :] = state
        beta, _, _, ratio, carry, ends, last = decays(i)
        keys, query = r.k[here, :], r.q[here, :]
        target = beta * (r.v[here, :] - carry * dot(keys, state, 1, 1))
        update = dot(r.inverses[here, :], target, 1, 0)
        r.u[here, :] = update
        weights = ratio * dot(query, keys, 1, 1)
        o = carry * dot(query, state, 1, 1) + dot(weights, update, 1, 0)
        r.o[here, :] = o
        state = last * state + dot(update * ends, keys, 0, 0)
        gate = r.proj[PAD + here.start : PAD + here.stop, c0:c1]
        mixed = o * inverse_rms(o, 1e-05) * r.out_gain[...] * (gate * jax.nn.sigmoid(gate))
        r.mixed_all[me_z, here, :] = mixed.astype(BF16)
        part = r.mixed_all.at[me_z, pl.ds(i * BLOCK, BLOCK), :]
        z_start(Z_MIXED + i, lambda p, part=part: part, part)
    g_out.step(1)
    g_d.finish(2)
    g_gu.finish(2)
    z_wait(Z_COT, lambda p: r.cot_all.at[block_rows(p), :])
    g_out.finish(2)

    ffn_gain_sum = jnp.zeros((1, D), F32)
    for c in chunks:
        for i in range(c.start // BLOCK, c.stop // BLOCK):
            z_wait(Z_MIXED + i, lambda p, i=i: r.mixed_all.at[p, pl.ds(i * BLOCK, BLOCK), :])
        total = r.x_all[c, :].astype(F32)
        for h in range(T):
            total = total + nt(r.mixed_all[h, c, :], r.w_out_all[h])
        r.resid[c, :] = total
        hhat = total * inverse_rms(total, 1e-06)
        r.n2[c, :] = (hhat * r.gain2[...]).astype(BF16)
        fgate = nn(r.n2[c, :], r.w_gu_all[:, :F])
        fup = nn(r.n2[c, :], r.w_gu_all[:, F:])
        dhidden = nn(r.cot_all[c, :], r.w_d_all[...])
        sigma = jax.nn.sigmoid(fgate)
        gated = fgate * sigma
        r.hidden[c, :] = (gated * fup).astype(BF16)
        r.dgu[c, F:] = (dhidden * gated).astype(BF16)
        r.dgu[c, :F] = (dhidden * fup * sigma * (1.0 + fgate * (1.0 - sigma))).astype(BF16)
        dn2 = nt(r.dgu[c, :], r.w_gu_all[...])
        r.dn2_send[c, :] = dn2.astype(BF16)
        z_start(
            Z_DN2,
            lambda p: r.dn2_send.at[block_rows(p), :],
            r.dn2_recv.at[me_z],
            range(c.start // R, c.stop // R),
        )
        total = r.resid[c, :]
        hhat = total * inverse_rms(total, 1e-06)
        ffn_gain_sum = ffn_gain_sum + jnp.sum(dn2 * hhat, 0, keepdims=True)
    r.small_z[me_z] = jnp.zeros((8, D), F32)
    r.small_z[me_z, 1:2, :] = ffn_gain_sum
    transpose_into(r.cot_all)
    weight_grad(r.hidden, slice(0, F), s_d, 0)
    s_d.start(0)
    transpose_into(r.n2)
    weight_grad(r.dgu, slice(0, F), s_gu, 0)
    weight_grad(r.dgu, slice(F, 2 * F), s_gu, F)
    s_gu.start(0)
    for c in chunks:
        r.y_send[c, :] = nt(r.hidden[c, :], r.w_d_all[...]).astype(BF16)
    z_wait(Z_DN2, lambda p: r.dn2_recv.at[p])

    def summed(own_send, received):
        total = own_send[own, :].astype(F32)
        for d in range(1, T):
            total = total + received[lax.rem(me_z + d, T)].astype(F32)
        return total

    def norm_back(total, gain, upstream):
        inverse = inverse_rms(total, 1e-06)
        hat = total * inverse
        e = upstream * gain
        return inverse * (e - hat * jnp.mean(e * hat, -1, keepdims=True))

    dresid = r.cot[...].astype(F32) + norm_back(
        r.resid[own, :], r.gain2[...], summed(r.dn2_send, r.dn2_recv)
    )
    r.dresid[...] = dresid
    r.dres_all[own, :] = dresid.astype(BF16)
    z_start(Z_DRES, lambda p: r.dres_all.at[own, :], r.dres_all.at[own, :])
    s_d.step(0)
    s_gu.step(0)
    z_wait(Z_DRES, lambda p: r.dres_all.at[block_rows(p), :])
    z_start(Z_Y, lambda p: r.y_send.at[block_rows(p), :], r.y_recv.at[me_z])
    transpose_into(r.dres_all)
    r.mixed_own[...] = r.mixed_all[me_z]
    weight_grad(r.mixed_own, slice(0, DV), s_out, 0)
    s_out.start(0)

    lane = lax.broadcasted_iota(jnp.int32, (1, LANES), 1)
    dstate = jnp.zeros((DV, DK), F32)
    out_gain_sum = jnp.zeros((1, DV), F32)
    conv_sums = [jnp.zeros((1, c0), F32) for _ in range(4)]
    a_log_sum = jnp.zeros((1, 1), F32)
    dt_sum = jnp.zeros((1, 1), F32)
    for i in reversed(range(blocks)):
        here = rows_of(i)
        base = PAD + i * BLOCK
        dmixed = nn(r.dres_all[here, :], r.w_out_all[me_z])
        gate = r.proj[base : base + BLOCK, c0:c1]
        o = r.o[here, :]
        inverse = inverse_rms(o, 1e-05)
        o_hat = o * inverse
        sg = jax.nn.sigmoid(gate)
        dgate = dmixed * (o_hat * r.out_gain[...]) * sg * (1.0 + gate * (1.0 - sg))
        r.dproj[here, c0:c1] = dgate.astype(BF16)
        dnormed = dmixed * (gate * sg)
        out_gain_sum = out_gain_sum + jnp.sum(dnormed * o_hat, 0, keepdims=True)
        e = dnormed * r.out_gain[...]
        grad = inverse * (e - o_hat * jnp.mean(e * o_hat, -1, keepdims=True))

        state = r.states[i * DV : (i + 1) * DV, :]
        beta, before, log_decay, scale, carried, ends, last = decays(i)
        keys, query, update = r.k[here, :], r.q[here, :], r.u[here, :]
        kk = dot(keys, keys, 1, 1)
        qk = dot(query, keys, 1, 1)
        key_state = dot(keys, state, 1, 1)
        query_state = dot(query, state, 1, 1)
        rest = r.v[here, :] - carried * key_state
        key_dstate = dot(keys, dstate, 1, 1)
        dupdate = dot(scale * qk, grad, 0, 0) + ends * key_dstate
        dends = jnp.sum(key_dstate * update, -1, keepdims=True)
        dweights = dot(grad, update, 1, 1)
        dqk = dweights * scale
        dtarget = dot(r.inverses[here, :], dupdate, 0, 0)
        dlower = jnp.where(row > column, -dot(dtarget, update, 1, 1), 0.0)
        lower_kk = dlower * kk
        dbeta = jnp.sum(dtarget * rest, -1, keepdims=True) + jnp.sum(
            lower_kk * scale, -1, keepdims=True
        )
        drest = beta * dtarget
        dv = drest
        dcarry = jnp.sum(grad * query_state - drest * key_state, -1, keepdims=True)
        dratio = dweights * qk + beta * lower_kk
        dkk = dlower * beta * scale
        dquery_state = carried * grad
        dkey_state = -carried * drest
        dq = dot(dquery_state, state, 1, 0) + dot(dqk, keys, 1, 0)
        dk = (
            dot(update * ends, dstate, 1, 0)
            + dot(dqk, query, 0, 0)
            + dot(dkey_state, state, 1, 0)
            + dot(dkk, keys, 1, 0)
            + dot(dkk, keys, 0, 0)
        )
        dlast = jnp.sum(jnp.sum(dstate * state, 0, keepdims=True), 1, keepdims=True)
        dstate = (
            last * dstate + dot(dquery_state, query, 0, 0) + dot(dkey_state, keys, 0, 0)
        )

        weight = dratio * scale
        ended = dends * ends
        at_last = (lax.broadcasted_iota(jnp.int32, (BLOCK, 1), 0) == BLOCK - 1).astype(F32)
        dcum = (
            jnp.sum(weight, 1, keepdims=True)
            - to_column(jnp.sum(weight, 0, keepdims=True))
            - ended
            + dcarry * carried
            + at_last * (jnp.sum(ended, 0, keepdims=True) + dlast * last)
        )
        dlog = jnp.sum(jnp.where(column >= row, to_row(dcum), 0.0), 1, keepdims=True)
        a_log_sum = a_log_sum + jnp.sum(dlog * log_decay, 0, keepdims=True)
        ddecay = dlog * -jnp.exp(r.a_log[...]) * jax.nn.sigmoid(before)
        dt_sum = dt_sum + jnp.sum(ddecay, 0, keepdims=True)
        dbeta_in = dbeta * beta * (1.0 - beta)
        r.dproj[here, c1:] = jnp.where(
            lane == 0, dbeta_in, jnp.where(lane == 1, ddecay, 0.0)
        ).astype(BF16)

        total = conv_total(i)
        st = jax.nn.sigmoid(total)
        active = total * st
        slope = st * (1.0 + total * (1.0 - st))
        q, k = active[:, :DK], active[:, DK : 2 * DK]
        rq = lax.rsqrt(jnp.sum(q * q, -1, keepdims=True) + 1e-06)
        rk = lax.rsqrt(jnp.sum(k * k, -1, keepdims=True) + 1e-06)
        dq = dq * DK ** (-0.5)
        dq = rq * (dq - q * (rq * rq * jnp.sum(dq * q, -1, keepdims=True)))
        dk = rk * (dk - k * (rk * rk * jnp.sum(dk * k, -1, keepdims=True)))
        r.dtot[here, :DK] = dq * slope[:, :DK]
        r.dtot[here, DK : 2 * DK] = dk * slope[:, DK : 2 * DK]
        r.dtot[here, 2 * DK :] = dv * slope[:, 2 * DK :]
        dtotal = r.dtot[here, :]
        now = shifted_segment(i, 0)
        conv_sums[3] = conv_sums[3] + jnp.sum(
            dtotal * r.proj[base : base + BLOCK, :c0], 0, keepdims=True
        )
        dmixer = r.conv_w[3:4, :] * dtotal
        for o_ in range(1, 4):
            same = (shifted_segment(i, -o_) == now).astype(F32)
            conv_sums[3 - o_] = conv_sums[3 - o_] + jnp.sum(
                dtotal * same * r.proj[base - o_ : base - o_ + BLOCK, :c0], 0, keepdims=True
            )
            later = (shifted_segment(i, o_) == now).astype(F32)
            dmixer = dmixer + r.conv_w[3 - o_ : 4 - o_, :] * (
                later * r.dtot[i * BLOCK + o_ : (i + 1) * BLOCK + o_, :]
            )
        r.dproj[here, :c0] = dmixer.astype(BF16)
        if i == blocks - 1:
            s_d.step(1)
            s_out.step(0)
        if i == blocks - 2:
            s_gu.step(1)
        if i == blocks - 3:
            s_out.step(1)

    attn_gain_sum = jnp.zeros((1, D), F32)
    for c in chunks:
        dn1 = nt(r.dproj[c, :], r.w_in_all[...])
        r.dn1_send[c, :] = dn1.astype(BF16)
        z_start(
            Z_DN1,
            lambda p: r.dn1_send.at[block_rows(p), :],
            r.dn1_recv.at[me_z],
            range(c.start // R, c.stop // R),
        )
        x = r.x_all[c, :].astype(F32)
        attn_gain_sum = attn_gain_sum + jnp.sum(dn1 * (x * inverse_rms(x, 1e-06)), 0, keepdims=True)
    r.small_z[me_z, 0:1, :] = attn_gain_sum
    r.small_z[me_z, 2:3, :DV] = out_gain_sum
    for t in range(4):
        r.small_z[me_z, 3 + t : 4 + t, :c0] = conv_sums[t]
    r.small_z[me_z, 7:8, :LANES] = jnp.where(lane == 0, a_log_sum, jnp.where(lane == 1, dt_sum, 0.0))
    z_start(Z_SMALL, lambda p: r.small_z.at[me_z], r.small_z.at[me_z])
    transpose_into(r.n1)
    weight_grad(r.dproj, slice(0, NI), s_in, 0)
    s_in.start(0)
    z_wait(Z_SMALL, lambda p: r.small_z.at[p])
    everywhere = r.small_z[0]
    for p in range(1, T):
        everywhere = everywhere + r.small_z[p]
    which = lax.broadcasted_iota(jnp.int32, (8, D), 0)
    small = jnp.where(which < 3, everywhere, r.small_z[me_z])

    def small_copy(level):
        return pltpu.make_async_remote_copy(
            src_ref=r.small_s.at[level],
            dst_ref=r.small_v.at[level],
            send_sem=r.a_send.at[level],
            recv_sem=r.a_recv.at[level],
            device_id={"dp": flipped([level])},
            device_id_type=MESH,
        )

    def small_start(level, value):
        r.small_s[level] = value
        small_copy(level).start()

    def small_step(level):
        small_copy(level).wait_recv()
        return r.small_s[level] + r.small_v[level]

    small_start(0, small)
    for level in range(2, bits):
        s_d.step(level)
        s_gu.step(level)
        s_out.step(level)
    z_wait(Z_Y, lambda p: r.y_recv.at[p])
    r.o_block[...] = (r.resid[own, :] + summed(r.y_send, r.y_recv)).astype(BF16)
    for level in range(bits):
        s_in.step(level)
        small = small_step(level)
        if level + 1 < bits:
            small_start(level + 1, small)
    r.o_small[...] = small
    z_wait(Z_DN1, lambda p: r.dn1_recv.at[p])
    r.o_input[...] = r.dresid[...] + norm_back(
        r.x[...].astype(F32), r.gain1[...], summed(r.dn1_send, r.dn1_recv)
    )

    for k, p, src in sends:

        @pl.when(p != me_z)
        def _():
            z_copy(k, p, src(p), src(p), me_z).wait_send()

    for gather in (g_in, g_gu, g_d, g_out):
        gather.drain()
    for reduce in (s_in, s_gu, s_d, s_out):
        reduce.drain()
    for level in range(bits):
        small_copy(level).wait_send()


def fused(T, N, c0, c1, args):
    x, w_in, w_gu, w_d, w_out = (args[n] for n in ("x", "w_in", "w_gu", "w_d", "w_out"))
    R, D = x.shape
    S, NI = w_in.shape
    F = w_d.shape[1]
    L = args["seg"].shape[1]
    bits = N.bit_length() - 1
    blocks = L // BLOCK
    outs = {
        "o_block": ((R, D), BF16),
        "o_input": ((R, D), F32),
        "o_in": ((S, NI), F32),
        "o_gu": ((S, 2 * F), F32),
        "o_d": ((S, F), F32),
        "o_out": ((S, DV), F32),
        "o_small": ((8, D), F32),
    }
    scratch = {
        "x_all": ((L, D), BF16),
        "cot_all": ((L, D), BF16),
        "w_in_all": ((D, NI), BF16),
        "w_gu_all": ((D, 2 * F), BF16),
        "w_d_all": ((D, F), BF16),
        "w_out_all": ((T, D, DV), BF16),
        "n1": ((L, D), BF16),
        "n2": ((L, D), BF16),
        "proj": ((PAD + L, NI), F32),
        "segc": ((PAD + L + PAD, 1), F32),
        "q": ((L, DK), F32),
        "k": ((L, DK), F32),
        "v": ((L, DV), F32),
        "ratio": ((L, BLOCK), F32),
        "inverses": ((L, BLOCK), F32),
        "states": ((blocks * DV, DK), F32),
        "u": ((L, DV), F32),
        "o": ((L, DV), F32),
        "mixed_all": ((T, L, DV), BF16),
        "mixed_own": ((L, DV), BF16),
        "resid": ((L, D), F32),
        "hidden": ((L, F), BF16),
        "dgu": ((L, 2 * F), BF16),
        "dn2_send": ((L, D), BF16),
        "dn2_recv": ((T, R, D), BF16),
        "y_send": ((L, D), BF16),
        "y_recv": ((T, R, D), BF16),
        "dn1_send": ((L, D), BF16),
        "dn1_recv": ((T, R, D), BF16),
        "dresid": ((R, D), F32),
        "dres_all": ((L, D), BF16),
        "dtot": ((L + PAD, c0), F32),
        "dproj": ((L, NI), BF16),
        "turned": ((D, L), BF16),
        "pair": ((2 * S, max(F, NI)), F32),
        "small_z": ((T, 8, D), F32),
        "small_s": ((bits, 8, D), F32),
        "small_v": ((bits, 8, D), F32),
    }
    for name, wide in (("in", NI), ("gu", 2 * F), ("d", F), ("out", DV)):
        scratch["k_" + name] = ((N // 2 * S, wide), F32)
        for level in range(bits):
            rows = (N >> (level + 1)) * S
            scratch["s_" + name + str(level)] = ((rows, wide), BF16)
            scratch["v_" + name + str(level)] = ((rows, wide), BF16)
    semaphores = {
        "z_send": (Z_MIXED + blocks, T),
        "z_recv": (Z_MIXED + blocks, T),
        "g_send": (4, N - 1),
        "g_recv": (4, N - 1),
        "r_send": (4, bits),
        "r_recv": (4, bits),
        "a_send": (bits,),
        "a_recv": (bits,),
    }
    names = list(args) + list(outs) + list(scratch) + list(semaphores)
    cfg = {"T": T, "N": N, "S": S, "R": R, "L": L, "D": D, "NI": NI, "F": F, "c0": c0, "c1": c1}
    vmem = pl.BlockSpec(memory_space=pltpu.VMEM)
    result = pl.pallas_call(
        functools.partial(kernel, cfg, names),
        out_shape=[jax.ShapeDtypeStruct(*leaf) for leaf in outs.values()],
        in_specs=[vmem] * len(args),
        out_specs=[vmem] * len(outs),
        scratch_shapes=[pltpu.VMEM(*leaf) for leaf in scratch.values()]
        + [pltpu.SemaphoreType.DMA(shape) for shape in semaphores.values()],
        compiler_params=pltpu.CompilerParams(
            collective_id=0, has_side_effects=True, vmem_limit_bytes=62 * 2**20
        ),
    )(*args.values())
    return dict(zip(outs, result))


def local(
    block_input,
    segment_ids,
    attention_norm_gain,
    w_qkv,
    w_og,
    w_beta,
    w_alpha,
    conv_weight,
    a_log,
    dt_bias,
    out_gain,
    w_out,
    ffn_gain,
    w_ffn_gate,
    w_ffn_up,
    w_ffn_down,
    cotangent,
):
    T, N = lax.axis_size("tensor"), lax.axis_size("dp")
    c0 = w_qkv.shape[1]
    c1 = c0 + w_og.shape[1]
    hidden_here = w_ffn_gate.shape[1]
    spare = -hidden_here % LANES
    shard = w_qkv.shape[0]

    def widened(array):
        return jnp.pad(array, ((0, 0), (0, spare)))

    args = {
        "x": block_input,
        "seg": segment_ids,
        "gain1": attention_norm_gain[None],
        "w_in": jnp.concatenate(
            [w_qkv, w_og, w_beta, w_alpha, jnp.zeros((shard, LANES - 2), BF16)], 1
        ),
        "w_gu": jnp.concatenate([widened(w_ffn_gate), widened(w_ffn_up)], 1),
        "w_d": widened(w_ffn_down.T),
        "w_out": w_out.T,
        "conv_w": conv_weight,
        "a_log": a_log[None],
        "dt_bias": dt_bias[None],
        "out_gain": out_gain[None],
        "gain2": ffn_gain[None],
        "cot": cotangent,
    }
    got = fused(T, N, c0, c1, args)
    small, in_grad, gu_grad = got["o_small"], got["o_in"], got["o_gu"]
    wide = gu_grad.shape[1] // 2
    return (
        got["o_block"],
        got["o_input"],
        small[0],
        in_grad[:, :c0],
        in_grad[:, c0:c1],
        in_grad[:, c1 : c1 + 1],
        in_grad[:, c1 + 1 : c1 + 2],
        small[3:7, :c0],
        small[7, 0:1],
        small[7, 1:2],
        small[2, : out_gain.shape[0]],
        got["o_out"].T,
        small[1],
        gu_grad[:, :hidden_here],
        gu_grad[:, wide : wide + hidden_here],
        got["o_d"][:, :hidden_here].T,
    )


def solution(mesh):
    rows = P(("dp", "tensor"), None)
    split = P("dp", "tensor")
    turned = P("tensor", "dp")
    placed = (
        rows, P("dp", None), P(), split, split, split, split, P(None, "tensor"), P("tensor"),
        P("tensor"), P(), turned, P(), split, split, turned, rows,
    )
    given = (
        rows, rows, P(), split, split, split, split, P(None, "tensor"), P("tensor"), P("tensor"),
        P(), turned, P(), split, split, turned,
    )
    return jax.shard_map(local, mesh=mesh, in_specs=placed, out_specs=given, check_vma=False)
```

```python
import functools

import jax
import jax.numpy as jnp
from jax import lax
from jax.experimental import pallas as pl
from jax.experimental.pallas import tpu as pltpu
from jax.sharding import PartitionSpec as P

DK = 128
DV = 256
BLOCK = 128
PAD = 8
LANES = 128
F32 = jnp.float32
BF16 = jnp.bfloat16
HIGHEST = lax.Precision.HIGHEST
MESH = pl.DeviceIdType.MESH


def contract(left, right, left_dim, right_dim):
    return lax.dot_general(
        left, right, (((left_dim,), (right_dim,)), ((), ())), preferred_element_type=F32
    )


def nn(left, right):
    return contract(left, right, 1, 0)


def nt(left, right):
    return contract(left, right, 1, 1)


def dot(left, right, left_dim, right_dim):
    return lax.dot_general(
        left,
        right,
        (((left_dim,), (right_dim,)), ((), ())),
        precision=HIGHEST,
        preferred_element_type=F32,
    )


def grid_index():
    row = lax.broadcasted_iota(jnp.int32, (BLOCK, BLOCK), 0)
    column = lax.broadcasted_iota(jnp.int32, (BLOCK, BLOCK), 1)
    return row, column


def to_row(column_vector):
    row, column = grid_index()
    return jnp.sum(jnp.where(row == column, column_vector, 0.0), 0, keepdims=True)


def to_column(row_vector):
    row, column = grid_index()
    return jnp.sum(jnp.where(row == column, row_vector, 0.0), 1, keepdims=True)


def unit_lower_inverses(lowers):
    row, column = grid_index()
    span = 1
    results = None
    while span < BLOCK:
        pair = (row // (2 * span) == column // (2 * span)) & (row // span != column // span)
        corners = [jnp.where(pair, lower, 0.0) for lower in lowers]
        if results is None:
            identity = (row == column).astype(F32)
            results = [identity - corner for corner in corners]
        else:
            halves = [dot(corner, result, 1, 0) for corner, result in zip(corners, results)]
            results = [result - dot(result, half, 1, 0) for result, half in zip(results, halves)]
        span = span * 2
    return results


def inverse_rms(rows, epsilon):
    return lax.rsqrt(jnp.mean(rows * rows, -1, keepdims=True) + epsilon)


def softplus(value):
    return jnp.maximum(value, 0.0) + jnp.log1p(jnp.exp(-jnp.abs(value)))


class Refs:
    def __init__(self, names, refs):
        for name, ref in zip(names, refs):
            setattr(self, name, ref)


Z_X, Z_COT, Z_WOUT, Z_DN2, Z_DRES, Z_Y, Z_DN1, Z_SMALL, Z_MIXED = range(9)


def kernel(cfg, names, *refs):
    r = Refs(names, refs)
    T, N, S, R, L, D = cfg["T"], cfg["N"], cfg["S"], cfg["R"], cfg["L"], cfg["D"]
    NI, F, HID, c0, c1, ca = (cfg[name] for name in ("NI", "F", "HID", "c0", "c1", "ca"))
    bits = N.bit_length() - 1
    blocks = L // BLOCK
    me_z = lax.axis_index("tensor")
    me_d = lax.axis_index("dp")
    sends = []

    def bit(b):
        return lax.rem(lax.div(me_d, 1 << b), 2)

    def flipped(which):
        place = me_d
        for b in which:
            place = place + (1 << b) * (1 - 2 * bit(b))
        return place

    barrier = pltpu.get_barrier_semaphore()
    for p in range(T):

        @pl.when(p != me_z)
        def _():
            pl.semaphore_signal(barrier, inc=1, device_id={"tensor": p}, device_id_type=MESH)

    for b in range(bits):
        pl.semaphore_signal(barrier, inc=1, device_id={"dp": flipped([b])}, device_id_type=MESH)

    far = T >= 3
    relays = ((0, 1, T - 2), (T - 1, T - 2, 1))

    def z_copy(k, device, src, dst, sent, received):
        return pltpu.make_async_remote_copy(
            src_ref=src,
            dst_ref=dst,
            send_sem=r.z_send.at[k, sent],
            recv_sem=r.z_recv.at[k, received],
            device_id={"tensor": device},
            device_id_type=MESH,
        )

    def z_start(condition, *copy):
        @pl.when(condition)
        def _():
            z_copy(*copy).start()

        sends.append((condition, copy))

    def z_take(condition, k, landing, received):
        @pl.when(condition)
        def _():
            z_copy(k, me_z, landing, landing, 0, received).wait_recv()

    def between(p):
        if far and p in (0, T - 1):
            return (me_z != 0) & (me_z != T - 1)
        return me_z != p

    def gather_start(k, place):
        def to(condition, p):
            z_start(condition, k, p, place(me_z), place(me_z), p, me_z)

        if far:
            to(me_z == 0, T - 2)
        for p in range(T):
            to(between(p) & (me_z != 0) if far and p == T - 2 else between(p), p)

    def gather_relay(k, place):
        if far:
            for n, (end, _, passing) in enumerate(relays):
                z_take(me_z == passing, k, place(end), end)
                z_start(me_z == passing, k, T - 1 - end, place(end), place(end), T + n, end)

    def gather_wait(k, place, then=None):
        for p in range(T):
            here = me_z != p
            for end, _, passing in relays if far else ():
                if end == p:
                    here = here & (me_z != passing)
            z_take(here, k, place(p), p)
            if then is not None:
                pl.when(me_z != p)(functools.partial(then, p))

    def rows_for(ref, p):
        return ref.at[pl.ds(p * R, R), :]

    def sum_start(k, send, recv, via, peers):
        for n, (end, near, _) in enumerate(relays if far else ()):
            p = T - 1 - end
            if p in peers:
                z_start(me_z == end, k, near, rows_for(send, p), via.at[n], p, T + n)
        for p in peers:
            direct = me_z != p
            for end, near, _ in relays if far else ():
                if p == T - 1 - end:
                    direct = direct & (me_z != end) & (me_z != near)
            z_start(direct, k, p, rows_for(send, p), recv.at[me_z], p, me_z)

    def sum_relay(k, send, recv, via):
        for n, (end, near, passing) in enumerate(relays if far else ()):
            p = T - 1 - end
            z_take(me_z == near, k, via.at[n], T + n)

            @pl.when(me_z == near)
            def _():
                rows = pl.ds(p * R, R)
                send[rows, :] = (send[rows, :].astype(F32) + via[n].astype(F32)).astype(BF16)

            z_start(me_z == near, k, p, rows_for(send, p), recv.at[near], p, near)

    def sum_clear(recv):
        for end, _, _ in relays if far else ():

            @pl.when(me_z == end)
            def _():
                recv[T - 1 - end] = jnp.zeros((R, D), BF16)

    def sum_wait(k, recv):
        for p in range(T):
            z_take(between(p), k, recv.at[p], p)

    class Gather:
        def __init__(self, index, place, order):
            self.index, self.place, self.order = index, place, order

        def copies(self, s, arriving):
            out = []
            for subset in range(1 << s):
                which = [self.order[t] for t in range(s) if subset >> t & 1]
                j = flipped(which + ([self.order[s]] if arriving else []))
                n = (1 << s) - 1 + subset
                out.append(
                    pltpu.make_async_remote_copy(
                        src_ref=self.place(j),
                        dst_ref=self.place(j),
                        send_sem=r.g_send.at[self.index, n],
                        recv_sem=r.g_recv.at[self.index, n],
                        device_id={"dp": flipped([self.order[s]])},
                        device_id_type=MESH,
                    )
                )
            return out

        def start(self, s):
            if s < bits:
                for copy in self.copies(s, False):
                    copy.start()

        def wait(self, s):
            if s < bits:
                for copy in self.copies(s, True):
                    copy.wait_recv()

        def step(self, s):
            self.wait(s)
            self.start(s + 1)

        def finish(self, s):
            for t in range(s, bits):
                self.step(t)

        def drain(self):
            for s in range(bits):
                for copy in self.copies(s, False):
                    copy.wait_send()

    upward = list(range(1, bits)) + [0]
    downward = list(reversed(range(1, bits))) + [0]

    def shard_of(ref, first=0, end=None):
        end = ref.shape[1] if end is None else end
        return lambda j: ref.at[pl.ds(pl.multiple_of(j * S, S), S), first:end]

    def shard_of3(ref):
        return lambda j: ref.at[:, pl.ds(pl.multiple_of(j * S, S), S), :]

    own_rows = pl.ds(pl.multiple_of(me_d * S, S), S)
    g_in = Gather(0, shard_of(r.w_in_all, 0, c0), upward)
    g_ig = Gather(4, shard_of(r.w_in_all, c0, NI), downward)
    g_gu = Gather(1, shard_of(r.w_gu_all), upward)
    g_d = Gather(2, shard_of(r.w_d_all), downward)
    g_out = Gather(3, shard_of3(r.w_out_all), upward)

    class Reduce:
        def __init__(self, index, keep, send, recv, out, order):
            self.index, self.keep, self.send, self.recv, self.out = index, keep, send, recv, out
            self.order = order

        def copy(self, level):
            return pltpu.make_async_remote_copy(
                src_ref=self.send[level],
                dst_ref=self.recv[level],
                send_sem=r.r_send.at[self.index, level],
                recv_sem=r.r_recv.at[self.index, level],
                device_id={"dp": flipped([self.order[level]])},
                device_id_type=MESH,
            )

        def start(self, level):
            self.copy(level).start()

        def step(self, level):
            self.copy(level).wait_recv()
            keep, recv = self.keep, self.recv[level]

            def part(j):
                rows = pl.ds(pl.multiple_of(j * S, S), S)
                return keep[rows, :] + recv[rows, :].astype(F32)

            if level + 1 == bits:
                self.out[...] = part(0)
                return
            half = N >> (level + 2)
            mine = bit(self.order[level + 1])
            low_first = self.order is reduce_up

            def body(q, carry):
                if low_first:
                    a, b = 2 * q + mine, 2 * q + 1 - mine
                else:
                    a, b = q + half * mine, q + half * (1 - mine)
                stay, leave = part(a), part(b)
                rows = pl.ds(pl.multiple_of(q * S, S), S)
                keep[rows, :] = stay
                self.send[level + 1][rows, :] = leave.astype(BF16)
                return carry

            lax.fori_loop(0, half, body, 0)
            self.start(level + 1)

        def drain(self):
            for level in range(bits):
                self.copy(level).wait_send()

    reduce_up = [0] + list(range(1, bits))
    reduce_down = [0] + list(reversed(range(1, bits)))

    def levels(prefix):
        return [getattr(r, prefix + str(level)) for level in range(bits)]

    s_a = Reduce(0, r.k_a, levels("s_a"), levels("v_a"), r.o_a, reduce_up)
    s_b = Reduce(4, r.k_b, levels("s_b"), levels("v_b"), r.o_b, reduce_down)
    s_og = Reduce(5, r.k_og, levels("s_og"), levels("v_og"), r.o_og, reduce_down)
    s_gu = Reduce(1, r.k_gu, levels("s_gu"), levels("v_gu"), r.o_gu, reduce_up)
    s_d = Reduce(2, r.k_d, levels("s_d"), levels("v_d"), r.o_d, reduce_down)
    s_out = Reduce(3, r.k_out, levels("s_out"), levels("v_out"), r.o_out, reduce_down)

    def transpose_into(source):
        for i in range(blocks):
            here = slice(i * BLOCK, (i + 1) * BLOCK)
            r.turned[:, here] = source[here, :].T

    def weight_grad(right, columns, sum_of, at):
        wide = columns.stop - columns.start

        def body(p, carry):
            pair = pl.ds(pl.multiple_of(p * 2 * S, 2 * S), 2 * S)
            rows = pl.ds(pl.multiple_of(p * S, S), S)
            r.pair[:, :wide] = nn(r.turned[pair, :], right[:, columns])
            mine, other = bit(0) * S, (1 - bit(0)) * S
            sum_of.keep[rows, at : at + wide] = r.pair[pl.ds(pl.multiple_of(mine, S), S), :wide]
            sum_of.send[0][rows, at : at + wide] = r.pair[
                pl.ds(pl.multiple_of(other, S), S), :wide
            ].astype(BF16)
            return carry

        lax.fori_loop(0, N // 2, body, 0)

    def block_rows(p):
        return pl.ds(p * R if isinstance(p, int) else pl.multiple_of(p * R, R), R)

    own = block_rows(me_z)

    def rows_place(ref):
        return lambda p: ref.at[block_rows(p), :]

    r.x_all[own, :] = r.x[...]
    r.w_in_all[own_rows, :c0] = r.w_qkv[...]
    r.w_in_all[own_rows, c0:c1] = r.w_og[...]
    place = lax.broadcasted_iota(jnp.int32, (LANES, S), 0)
    both = jnp.where(place == 0, r.w_beta[...].astype(F32), 0.0)
    both = jnp.where(place == 1, r.w_alpha[...].astype(F32), both)
    r.w_in_all[own_rows, c1:] = both.T.astype(BF16)
    pl.semaphore_wait(barrier, T - 1 + bits)
    gather_start(Z_X, rows_place(r.x_all))
    g_in.start(0)
    g_ig.start(0)
    r.w_d_all[own_rows, :] = jnp.zeros((S, F), BF16)
    r.w_gu_all[own_rows, :] = jnp.zeros((S, 2 * F), BF16)
    r.w_d_all[own_rows, :HID] = r.w_down[...].T
    r.w_out_all[me_z, own_rows, :] = r.w_out[...].T
    r.w_gu_all[own_rows, :HID] = r.w_gate[...].T
    r.w_gu_all[own_rows, F : F + HID] = r.w_up[...].T
    r.cot_all[own, :] = r.cot[...]
    for recv in (r.dn2_recv, r.y_recv, r.dn1_recv):
        sum_clear(recv)

    def first_norm(rows):
        x = r.x_all[rows, :].astype(F32)
        r.n1[rows, :] = (x * inverse_rms(x, 1e-06) * r.gain1[...]).astype(BF16)

    g_ig.step(0)
    g_in.step(0)
    first_norm(own)
    segment = r.seg[...].astype(F32)
    r.segc[0:PAD, :] = jnp.full((PAD, 1), -1.0, F32)
    r.segc[PAD + L :, :] = jnp.full((PAD, 1), -2.0, F32)
    for i in range(blocks):
        r.segc[PAD + i * BLOCK : PAD + (i + 1) * BLOCK, :] = to_column(
            segment[:, i * BLOCK : (i + 1) * BLOCK]
        )
    r.proj[0:PAD, :] = jnp.zeros((PAD, NI), F32)
    r.dtot[L:, :] = jnp.zeros((PAD, c0), F32)
    g_ig.step(1)
    g_in.step(1)
    g_d.start(0)
    g_gu.start(0)

    def out_place(p):
        return r.w_out_all.at[p, own_rows, :]

    gather_relay(Z_X, rows_place(r.x_all))
    gather_wait(Z_X, rows_place(r.x_all))
    gather_start(Z_WOUT, out_place)
    gather_start(Z_COT, rows_place(r.cot_all))
    for p in range(T):
        pl.when(me_z != p)(functools.partial(first_norm, block_rows(p)))
    g_ig.finish(2)
    g_in.finish(2)
    g_d.step(0)
    g_gu.step(0)
    chunk = 2 * R
    chunks = [slice(i * chunk, (i + 1) * chunk) for i in range(L // chunk)]
    for c in chunks:
        r.proj[PAD + c.start : PAD + c.stop, :] = nn(r.n1[c, :], r.w_in_all[...])
    gather_relay(Z_WOUT, out_place)
    row, column = grid_index()
    inclusive = row >= column

    def shifted_segment(i, o):
        return r.segc[PAD + i * BLOCK + o : PAD + (i + 1) * BLOCK + o, :]

    def conv_total(i):
        base = PAD + i * BLOCK
        now = shifted_segment(i, 0)
        total = r.conv_w[3:4, :] * r.proj[base : base + BLOCK, :c0]
        for o in range(1, 4):
            same = (shifted_segment(i, -o) == now).astype(F32)
            total = total + r.conv_w[3 - o : 4 - o, :] * (
                r.proj[base - o : base - o + BLOCK, :c0] * same
            )
        return total

    def decays(i):
        base = PAD + i * BLOCK
        both = r.proj[base : base + BLOCK, c1:]
        beta = jax.nn.sigmoid(both[:, 0:1])
        before = both[:, 1:2] + r.dt_bias[...]
        log_decay = -jnp.exp(r.a_log[...]) * softplus(before)
        cum_row = jnp.sum(jnp.where(row <= column, log_decay, 0.0), 0, keepdims=True)
        cum = to_column(cum_row)
        seg_col = shifted_segment(i, 0)
        seg_row = segment[:, i * BLOCK : (i + 1) * BLOCK]
        keep = (seg_col == seg_row) & inclusive
        ratio = jnp.where(keep, jnp.exp(jnp.where(keep, cum - cum_row, 0.0)), 0.0)
        first = PAD + i * BLOCK
        carry = jnp.where(seg_col == r.segc[first - 1 : first, :], jnp.exp(cum), 0.0)
        ends = to_column(ratio[BLOCK - 1 : BLOCK, :])
        last = carry[BLOCK - 1 : BLOCK, :]
        return beta, before, log_decay, ratio, carry, ends, last

    def rows_of(i):
        return slice(i * BLOCK, (i + 1) * BLOCK)

    def mixed_place(i):
        return lambda p: r.mixed_all.at[p, pl.ds(i * BLOCK, BLOCK), :]

    lowers = []
    for i in range(blocks):
        here = rows_of(i)
        total = conv_total(i)
        active = total * jax.nn.sigmoid(total)
        q, k, v = active[:, :DK], active[:, DK : 2 * DK], active[:, 2 * DK :]
        q = q * lax.rsqrt(jnp.sum(q * q, -1, keepdims=True) + 1e-06) * DK ** (-0.5)
        k = k * lax.rsqrt(jnp.sum(k * k, -1, keepdims=True) + 1e-06)
        r.q[here, :], r.k[here, :], r.v[here, :] = q, k, v
        beta, _, _, ratio, carry, ends, last = decays(i)
        r.ratio[here, :] = ratio
        lowers.append(jnp.where(row > column, beta * ratio * dot(k, k, 1, 1), 0.0))
        if i == 1:
            gather_wait(Z_WOUT, out_place)
            g_out.start(0)
    g_d.step(1)
    inverse_list = unit_lower_inverses(lowers)
    for i in range(blocks):
        r.inverses[rows_of(i), :] = inverse_list[i]
    state = jnp.zeros((DV, DK), F32)
    for i in range(blocks):
        here = rows_of(i)
        r.states[i * DV : (i + 1) * DV, :] = state
        beta, _, _, ratio, carry, ends, last = decays(i)
        keys, query = r.k[here, :], r.q[here, :]
        target = beta * (r.v[here, :] - carry * dot(keys, state, 1, 1))
        update = dot(r.inverses[here, :], target, 1, 0)
        r.u[here, :] = update
        weights = ratio * dot(query, keys, 1, 1)
        o = carry * dot(query, state, 1, 1) + dot(weights, update, 1, 0)
        r.o[here, :] = o
        state = last * state + dot(update * ends, keys, 0, 0)
        gate = r.proj[PAD + here.start : PAD + here.stop, c0:c1]
        mixed = o * inverse_rms(o, 1e-05) * r.out_gain[...] * (gate * jax.nn.sigmoid(gate))
        r.mixed_all[me_z, here, :] = mixed.astype(BF16)
        gather_start(Z_MIXED + i, mixed_place(i))
    gather_relay(Z_COT, rows_place(r.cot_all))
    g_out.step(0)
    g_gu.step(1)
    g_d.finish(2)
    for i in range(chunk // BLOCK):
        gather_relay(Z_MIXED + i, mixed_place(i))
    g_out.step(1)
    g_gu.finish(2)
    g_out.finish(2)
    gather_wait(Z_COT, rows_place(r.cot_all))

    ffn_gain_sum = jnp.zeros((1, D), F32)
    for c in chunks:
        of_chunk = range(c.start // BLOCK, c.stop // BLOCK)
        for i in of_chunk:
            gather_wait(Z_MIXED + i, mixed_place(i))
        total = r.x_all[c, :].astype(F32)
        for h in range(T):
            total = total + nt(r.mixed_all[h, c, :], r.w_out_all[h])
        r.resid[c, :] = total
        hhat = total * inverse_rms(total, 1e-06)
        r.n2[c, :] = (hhat * r.gain2[...]).astype(BF16)
        fgate = nn(r.n2[c, :], r.w_gu_all[:, :F])
        fup = nn(r.n2[c, :], r.w_gu_all[:, F:])
        for i in range(c.stop // BLOCK, blocks) if c.start == 0 else ():
            gather_relay(Z_MIXED + i, mixed_place(i))
        dhidden = nn(r.cot_all[c, :], r.w_d_all[...])
        sigma = jax.nn.sigmoid(fgate)
        gated = fgate * sigma
        r.hidden[c, :] = (gated * fup).astype(BF16)
        r.dgu[c, F:] = (dhidden * gated).astype(BF16)
        r.dgu[c, :F] = (dhidden * fup * sigma * (1.0 + fgate * (1.0 - sigma))).astype(BF16)
        dn2 = nt(r.dgu[c, :], r.w_gu_all[...])
        r.dn2_send[c, :] = dn2.astype(BF16)
        sum_start(Z_DN2, r.dn2_send, r.dn2_recv, r.dn2_via, range(c.start // R, c.stop // R))
        total = r.resid[c, :]
        hhat = total * inverse_rms(total, 1e-06)
        ffn_gain_sum = ffn_gain_sum + jnp.sum(dn2 * hhat, 0, keepdims=True)
    r.small_z[me_z] = jnp.zeros((8, D), F32)
    r.small_z[me_z, 1:2, :] = ffn_gain_sum
    transpose_into(r.cot_all)
    weight_grad(r.hidden, slice(0, F), s_d, 0)
    s_d.start(0)
    sum_relay(Z_DN2, r.dn2_send, r.dn2_recv, r.dn2_via)
    transpose_into(r.n2)
    weight_grad(r.dgu, slice(0, F), s_gu, 0)
    weight_grad(r.dgu, slice(F, 2 * F), s_gu, F)
    s_gu.start(0)
    s_d.step(0)
    for c in chunks:
        r.y_send[c, :] = nt(r.hidden[c, :], r.w_d_all[...]).astype(BF16)
    s_gu.step(0)
    sum_wait(Z_DN2, r.dn2_recv)

    def summed(own_send, received):
        total = own_send[own, :].astype(F32)
        for d in range(1, T):
            total = total + received[lax.rem(me_z + d, T)].astype(F32)
        return total

    def norm_back(total, gain, upstream):
        inverse = inverse_rms(total, 1e-06)
        hat = total * inverse
        e = upstream * gain
        return inverse * (e - hat * jnp.mean(e * hat, -1, keepdims=True))

    dresid = r.cot[...].astype(F32) + norm_back(
        r.resid[own, :], r.gain2[...], summed(r.dn2_send, r.dn2_recv)
    )
    r.dresid[...] = dresid
    r.dres_all[own, :] = dresid.astype(BF16)
    gather_start(Z_DRES, rows_place(r.dres_all))
    s_d.step(1)
    gather_relay(Z_DRES, rows_place(r.dres_all))
    gather_wait(Z_DRES, rows_place(r.dres_all))
    sum_start(Z_Y, r.y_send, r.y_recv, r.y_via, range(T))
    transpose_into(r.dres_all)
    weight_grad(r.mixed_all.at[me_z], slice(0, DV), s_out, 0)
    s_out.start(0)

    out_gain_sum = jnp.zeros((1, DV), F32)
    for i in range(blocks):
        here = rows_of(i)
        base = PAD + i * BLOCK
        dmixed = nn(r.dres_all[here, :], r.w_out_all[me_z])
        gate = r.proj[base : base + BLOCK, c0:c1]
        o = r.o[here, :]
        inverse = inverse_rms(o, 1e-05)
        o_hat = o * inverse
        sg = jax.nn.sigmoid(gate)
        dgate = dmixed * (o_hat * r.out_gain[...]) * sg * (1.0 + gate * (1.0 - sg))
        r.dproj[here, c0:c1] = dgate.astype(BF16)
        dnormed = dmixed * (gate * sg)
        out_gain_sum = out_gain_sum + jnp.sum(dnormed * o_hat, 0, keepdims=True)
        e = dnormed * r.out_gain[...]
        r.o[here, :] = inverse * (e - o_hat * jnp.mean(e * o_hat, -1, keepdims=True))
    s_out.step(0)
    transpose_into(r.n1)
    weight_grad(r.dproj, slice(c0, c1), s_og, 0)
    s_og.start(0)
    lane = lax.broadcasted_iota(jnp.int32, (1, LANES), 1)
    dstate = jnp.zeros((DV, DK), F32)
    conv_sums = [jnp.zeros((1, c0), F32) for _ in range(4)]
    a_log_sum = jnp.zeros((1, 1), F32)
    dt_sum = jnp.zeros((1, 1), F32)
    for i in reversed(range(blocks)):
        here = rows_of(i)
        base = PAD + i * BLOCK
        grad = r.o[here, :]
        state = r.states[i * DV : (i + 1) * DV, :]
        beta, before, log_decay, scale, carried, ends, last = decays(i)
        keys, query, update = r.k[here, :], r.q[here, :], r.u[here, :]
        kk = dot(keys, keys, 1, 1)
        qk = dot(query, keys, 1, 1)
        key_state = dot(keys, state, 1, 1)
        query_state = dot(query, state, 1, 1)
        rest = r.v[here, :] - carried * key_state
        key_dstate = dot(keys, dstate, 1, 1)
        dupdate = dot(scale * qk, grad, 0, 0) + ends * key_dstate
        dends = jnp.sum(key_dstate * update, -1, keepdims=True)
        dweights = dot(grad, update, 1, 1)
        dqk = dweights * scale
        dtarget = dot(r.inverses[here, :], dupdate, 0, 0)
        dlower = jnp.where(row > column, -dot(dtarget, update, 1, 1), 0.0)
        lower_kk = dlower * kk
        dbeta = jnp.sum(dtarget * rest, -1, keepdims=True) + jnp.sum(
            lower_kk * scale, -1, keepdims=True
        )
        drest = beta * dtarget
        dv = drest
        dcarry = jnp.sum(grad * query_state - drest * key_state, -1, keepdims=True)
        dratio = dweights * qk + beta * lower_kk
        dkk = dlower * beta * scale
        dquery_state = carried * grad
        dkey_state = -carried * drest
        dq = dot(dquery_state, state, 1, 0) + dot(dqk, keys, 1, 0)
        dk = (
            dot(update * ends, dstate, 1, 0)
            + dot(dqk, query, 0, 0)
            + dot(dkey_state, state, 1, 0)
            + dot(dkk, keys, 1, 0)
            + dot(dkk, keys, 0, 0)
        )
        dlast = jnp.sum(jnp.sum(dstate * state, 0, keepdims=True), 1, keepdims=True)
        dstate = (
            last * dstate + dot(dquery_state, query, 0, 0) + dot(dkey_state, keys, 0, 0)
        )

        weight = dratio * scale
        ended = dends * ends
        at_last = (lax.broadcasted_iota(jnp.int32, (BLOCK, 1), 0) == BLOCK - 1).astype(F32)
        dcum = (
            jnp.sum(weight, 1, keepdims=True)
            - to_column(jnp.sum(weight, 0, keepdims=True))
            - ended
            + dcarry * carried
            + at_last * (jnp.sum(ended, 0, keepdims=True) + dlast * last)
        )
        dlog = jnp.sum(jnp.where(column >= row, to_row(dcum), 0.0), 1, keepdims=True)
        a_log_sum = a_log_sum + jnp.sum(dlog * log_decay, 0, keepdims=True)
        ddecay = dlog * -jnp.exp(r.a_log[...]) * jax.nn.sigmoid(before)
        dt_sum = dt_sum + jnp.sum(ddecay, 0, keepdims=True)
        dbeta_in = dbeta * beta * (1.0 - beta)
        r.dproj[here, c1:] = jnp.where(
            lane == 0, dbeta_in, jnp.where(lane == 1, ddecay, 0.0)
        ).astype(BF16)

        total = conv_total(i)
        st = jax.nn.sigmoid(total)
        active = total * st
        slope = st * (1.0 + total * (1.0 - st))
        q, k = active[:, :DK], active[:, DK : 2 * DK]
        rq = lax.rsqrt(jnp.sum(q * q, -1, keepdims=True) + 1e-06)
        rk = lax.rsqrt(jnp.sum(k * k, -1, keepdims=True) + 1e-06)
        dq = dq * DK ** (-0.5)
        dq = rq * (dq - q * (rq * rq * jnp.sum(dq * q, -1, keepdims=True)))
        dk = rk * (dk - k * (rk * rk * jnp.sum(dk * k, -1, keepdims=True)))
        r.dtot[here, :DK] = dq * slope[:, :DK]
        r.dtot[here, DK : 2 * DK] = dk * slope[:, DK : 2 * DK]
        r.dtot[here, 2 * DK :] = dv * slope[:, 2 * DK :]
        dtotal = r.dtot[here, :]
        now = shifted_segment(i, 0)
        conv_sums[3] = conv_sums[3] + jnp.sum(
            dtotal * r.proj[base : base + BLOCK, :c0], 0, keepdims=True
        )
        dmixer = r.conv_w[3:4, :] * dtotal
        for o_ in range(1, 4):
            same = (shifted_segment(i, -o_) == now).astype(F32)
            conv_sums[3 - o_] = conv_sums[3 - o_] + jnp.sum(
                dtotal * same * r.proj[base - o_ : base - o_ + BLOCK, :c0], 0, keepdims=True
            )
            later = (shifted_segment(i, o_) == now).astype(F32)
            dmixer = dmixer + r.conv_w[3 - o_ : 4 - o_, :] * (
                later * r.dtot[i * BLOCK + o_ : (i + 1) * BLOCK + o_, :]
            )
        r.dproj[here, :c0] = dmixer.astype(BF16)
        if i == blocks - 1:
            s_og.step(0)
            s_out.step(1)
        if i == blocks - 2:
            s_gu.step(1)
            s_d.step(2)
        if i == blocks - 3:
            s_og.step(1)
            s_out.step(2)
    sum_relay(Z_Y, r.y_send, r.y_recv, r.y_via)

    attn_gain_sum = jnp.zeros((1, D), F32)
    for c in chunks:
        dn1 = nt(r.dproj[c, :], r.w_in_all[...])
        r.n2[c, :] = dn1.astype(BF16)
        sum_start(Z_DN1, r.n2, r.dn1_recv, r.dn1_via, range(c.start // R, c.stop // R))
        x = r.x_all[c, :].astype(F32)
        attn_gain_sum = attn_gain_sum + jnp.sum(dn1 * (x * inverse_rms(x, 1e-06)), 0, keepdims=True)
    r.small_z[me_z, 0:1, :] = attn_gain_sum
    r.small_z[me_z, 2:3, :DV] = out_gain_sum
    for t in range(4):
        r.small_z[me_z, 3 + t : 4 + t, :c0] = conv_sums[t]
    r.small_z[me_z, 7:8, :LANES] = jnp.where(lane == 0, a_log_sum, jnp.where(lane == 1, dt_sum, 0.0))
    for p in range(T):
        z_start(me_z != p, Z_SMALL, p, r.small_z.at[me_z], r.small_z.at[me_z], p, me_z)
    weight_grad(r.dproj, slice(0, ca), s_a, 0)
    s_a.start(0)
    weight_grad(r.dproj, slice(ca, c0), s_b, 0)
    weight_grad(r.dproj, slice(c1, NI), s_b, c0 - ca)
    s_b.start(0)
    for p in range(T):
        z_take(me_z != p, Z_SMALL, r.small_z.at[p], p)
    everywhere = r.small_z[0]
    for p in range(1, T):
        everywhere = everywhere + r.small_z[p]
    which = lax.broadcasted_iota(jnp.int32, (8, D), 0)
    small = jnp.where(which < 3, everywhere, r.small_z[me_z])

    def small_copy(level):
        return pltpu.make_async_remote_copy(
            src_ref=r.small_s.at[level],
            dst_ref=r.small_v.at[level],
            send_sem=r.a_send.at[level],
            recv_sem=r.a_recv.at[level],
            device_id={"dp": flipped([level])},
            device_id_type=MESH,
        )

    def small_start(level, value):
        r.small_s[level] = value
        small_copy(level).start()

    def small_step(level):
        small_copy(level).wait_recv()
        return r.small_s[level] + r.small_v[level]

    small_start(0, small)
    s_a.step(0)
    s_b.step(0)
    sum_relay(Z_DN1, r.n2, r.dn1_recv, r.dn1_via)
    for level in range(2, bits):
        s_gu.step(level)
        s_og.step(level)
        if level > 2:
            s_d.step(level)
            s_out.step(level)
    for level in range(bits):
        small = small_step(level)
        if level + 1 < bits:
            small_start(level + 1, small)
        if level > 0:
            s_b.step(level)
            s_a.step(level)
    sum_wait(Z_Y, r.y_recv)
    r.o_block[...] = (r.resid[own, :] + summed(r.y_send, r.y_recv)).astype(BF16)
    r.o_small[...] = small
    sum_wait(Z_DN1, r.dn1_recv)
    r.o_input[...] = r.dresid[...] + norm_back(
        r.x[...].astype(F32), r.gain1[...], summed(r.n2, r.dn1_recv)
    )

    for condition, copy in sends:

        @pl.when(condition)
        def _():
            z_copy(*copy).wait_send()

    for gather in (g_in, g_ig, g_gu, g_d, g_out):
        gather.drain()
    for reduce in (s_a, s_b, s_og, s_gu, s_d, s_out):
        reduce.drain()
    for level in range(bits):
        small_copy(level).wait_send()


def unpack(cfg, parts, *refs):
    count = len(parts)
    given, outs, here, sems = refs[:count], refs[count:-count - 1], refs[-count - 1 : -1], refs[-1]
    (block, inputs, attn, qkv, og, beta, alpha, conv, a_log, dt, gain, out, ffn, gate, up, down) = outs
    c0, ca, HID, F = cfg["c0"], cfg["ca"], cfg["HID"], cfg["F"]
    copies = [
        pltpu.make_async_copy(source, place, sems.at[n])
        for n, (source, place) in enumerate(zip(given, here))
    ]
    for copy in copies:
        copy.start()
    g = Refs(["h" + part[1:] for part in parts], here)
    arrived = dict(zip(parts, copies))
    arrived["o_gu"].wait()
    gate[...] = g.h_gu[:, :F].T[:HID, :]
    up[...] = g.h_gu[:, F:].T[:HID, :]
    arrived["o_d"].wait()
    down[...] = g.h_d[...].T[:HID, :]
    arrived["o_a"].wait()
    qkv[:, :ca] = g.h_a[...]
    arrived["o_b"].wait()
    qkv[:, ca:] = g.h_b[:, : c0 - ca]
    both = g.h_b[:, c0 - ca :].T
    beta[...] = both[0:1, :]
    alpha[...] = both[1:2, :]
    arrived["o_og"].wait()
    og[...] = g.h_og[...]
    arrived["o_small"].wait()
    attn[...] = g.h_small[0:1, :]
    ffn[...] = g.h_small[1:2, :]
    gain[...] = g.h_small[2:3, : gain.shape[1]]
    conv[...] = g.h_small[3:7, :c0]
    a_log[...] = g.h_small[7:8, 0:1]
    dt[...] = g.h_small[7:8, 1:2]
    arrived["o_out"].wait()
    out[...] = g.h_out[...].T
    arrived["o_block"].wait()
    block[...] = g.h_block[...]
    arrived["o_input"].wait()
    inputs[...] = g.h_input[...]


def fused(T, N, c0, c1, args):
    R, D = args["x"].shape
    S = args["w_qkv"].shape[0]
    NI = c1 + LANES
    HID = args["w_down"].shape[0]
    F = HID + -HID % LANES
    L = args["seg"].shape[1]
    ca = c0 - LANES
    wides = {"a": ca, "b": NI - ca - (c1 - c0), "og": c1 - c0, "gu": 2 * F, "d": F, "out": DV}
    bits = N.bit_length() - 1
    blocks = L // BLOCK
    outs = {
        "o_block": ((R, D), BF16),
        "o_input": ((R, D), F32),
        **{"o_" + name: ((S, wide), F32) for name, wide in wides.items()},
        "o_small": ((8, D), F32),
    }
    scratch = {
        "x_all": ((L, D), BF16),
        "cot_all": ((L, D), BF16),
        "w_in_all": ((D, NI), BF16),
        "w_gu_all": ((D, 2 * F), BF16),
        "w_d_all": ((D, F), BF16),
        "w_out_all": ((T, D, DV), BF16),
        "n1": ((L, D), BF16),
        "n2": ((L, D), BF16),
        "proj": ((PAD + L, NI), F32),
        "segc": ((PAD + L + PAD, 1), F32),
        "q": ((L, DK), F32),
        "k": ((L, DK), F32),
        "v": ((L, DV), F32),
        "ratio": ((L, BLOCK), F32),
        "inverses": ((L, BLOCK), F32),
        "states": ((blocks * DV, DK), F32),
        "u": ((L, DV), F32),
        "o": ((L, DV), F32),
        "mixed_all": ((T, L, DV), BF16),
        "resid": ((L, D), F32),
        "hidden": ((L, F), BF16),
        "dgu": ((L, 2 * F), BF16),
        "dn2_send": ((L, D), BF16),
        "dn2_recv": ((T, R, D), BF16),
        "dn2_via": ((2, R, D), BF16),
        "y_send": ((L, D), BF16),
        "y_recv": ((T, R, D), BF16),
        "y_via": ((2, R, D), BF16),
        "dn1_recv": ((T, R, D), BF16),
        "dn1_via": ((2, R, D), BF16),
        "dresid": ((R, D), F32),
        "dres_all": ((L, D), BF16),
        "dtot": ((L + PAD, c0), F32),
        "dproj": ((L, NI), BF16),
        "turned": ((D, L), BF16),
        "pair": ((2 * S, max(F, ca)), F32),
        "small_z": ((T, 8, D), F32),
        "small_s": ((bits, 8, D), F32),
        "small_v": ((bits, 8, D), F32),
    }
    for name, wide in wides.items():
        scratch["k_" + name] = ((N // 2 * S, wide), F32)
        for level in range(bits):
            rows = (N >> (level + 1)) * S
            scratch["s_" + name + str(level)] = ((rows, wide), BF16)
            scratch["v_" + name + str(level)] = ((rows, wide), BF16)
    semaphores = {
        "z_send": (Z_MIXED + blocks, T + 2),
        "z_recv": (Z_MIXED + blocks, T + 2),
        "g_send": (5, N - 1),
        "g_recv": (5, N - 1),
        "r_send": (6, bits),
        "r_recv": (6, bits),
        "a_send": (bits,),
        "a_recv": (bits,),
    }
    names = list(args) + list(outs) + list(scratch) + list(semaphores)
    cfg = {"T": T, "N": N, "S": S, "R": R, "L": L, "D": D, "NI": NI, "F": F}
    cfg.update({"HID": HID, "c0": c0, "c1": c1, "ca": ca})
    vmem = pl.BlockSpec(memory_space=pltpu.VMEM)
    result = pl.pallas_call(
        functools.partial(kernel, cfg, names),
        out_shape=[jax.ShapeDtypeStruct(*leaf) for leaf in outs.values()],
        in_specs=[vmem] * len(args),
        out_specs=[vmem] * len(outs),
        scratch_shapes=[pltpu.VMEM(*leaf) for leaf in scratch.values()]
        + [pltpu.SemaphoreType.DMA(shape) for shape in semaphores.values()],
        compiler_params=pltpu.CompilerParams(
            collective_id=0, has_side_effects=True, vmem_limit_bytes=62 * 2**20
        ),
    )(*args.values())
    got = dict(zip(outs, result))
    final = (
        ((R, D), BF16), ((R, D), F32), ((1, D), F32), ((S, c0), F32), ((S, c1 - c0), F32),
        ((1, S), F32), ((1, S), F32), (args["conv_w"].shape, F32), ((1, 1), F32), ((1, 1), F32),
        (args["out_gain"].shape, F32), ((DV, S), F32), ((1, D), F32), ((HID, S), F32),
        ((HID, S), F32), ((HID, S), F32),
    )
    parts = ("o_gu", "o_d", "o_a", "o_b", "o_og", "o_small", "o_out", "o_block", "o_input")
    return pl.pallas_call(
        functools.partial(unpack, cfg, parts),
        out_shape=[jax.ShapeDtypeStruct(*leaf) for leaf in final],
        in_specs=[pl.BlockSpec(memory_space=pl.ANY)] * len(parts),
        out_specs=[vmem] * len(final),
        scratch_shapes=[pltpu.VMEM(*outs[part]) for part in parts]
        + [pltpu.SemaphoreType.DMA((len(parts),))],
        compiler_params=pltpu.CompilerParams(vmem_limit_bytes=62 * 2**20),
    )(*[got[part] for part in parts])


def local(
    block_input,
    segment_ids,
    attention_norm_gain,
    w_qkv,
    w_og,
    w_beta,
    w_alpha,
    conv_weight,
    a_log,
    dt_bias,
    out_gain,
    w_out,
    ffn_gain,
    w_ffn_gate,
    w_ffn_up,
    w_ffn_down,
    cotangent,
):
    T, N = lax.axis_size("tensor"), lax.axis_size("dp")
    c0 = w_qkv.shape[1]
    c1 = c0 + w_og.shape[1]
    args = {
        "x": block_input,
        "seg": segment_ids,
        "gain1": attention_norm_gain[None],
        "w_qkv": w_qkv,
        "w_og": w_og,
        "w_beta": w_beta.T,
        "w_alpha": w_alpha.T,
        "w_gate": w_ffn_gate.T,
        "w_up": w_ffn_up.T,
        "w_down": w_ffn_down,
        "w_out": w_out,
        "conv_w": conv_weight,
        "a_log": a_log[None],
        "dt_bias": dt_bias[None],
        "out_gain": out_gain[None],
        "gain2": ffn_gain[None],
        "cot": cotangent,
    }
    (block, inputs, attn, qkv, og, beta, alpha, conv, a_log, dt, gain, out, ffn, gate, up, down) = fused(
        T, N, c0, c1, args
    )
    return (
        block, inputs, attn[0], qkv, og, beta.T, alpha.T, conv, a_log[0], dt[0], gain[0], out,
        ffn[0], gate.T, up.T, down,
    )


def solution(mesh):
    rows = P(("dp", "tensor"), None)
    split = P("dp", "tensor")
    turned = P("tensor", "dp")
    placed = (
        rows, P("dp", None), P(), split, split, split, split, P(None, "tensor"), P("tensor"),
        P("tensor"), P(), turned, P(), split, split, turned, rows,
    )
    given = (
        rows, rows, P(), split, split, split, split, P(None, "tensor"), P("tensor"), P("tensor"),
        P(), turned, P(), split, split, turned,
    )
    return jax.shard_map(local, mesh=mesh, in_specs=placed, out_specs=given, check_vma=False)
```

```python
import functools

import jax
import jax.numpy as jnp
from jax import lax
from jax.experimental import pallas as pl
from jax.experimental.pallas import tpu as pltpu
from jax.sharding import PartitionSpec as P

DK = 128
DV = 256
BLOCK = 128
PAD = 8
LANES = 128
F32 = jnp.float32
BF16 = jnp.bfloat16
MESH = pl.DeviceIdType.MESH


def contract(left, right, left_dim, right_dim):
    return lax.dot_general(
        left, right, (((left_dim,), (right_dim,)), ((), ())), preferred_element_type=F32
    )


def nn(left, right):
    return contract(left, right, 1, 0)


def nt(left, right):
    return contract(left, right, 1, 1)


def halves(value):
    high = value.astype(BF16)
    return high, (value - high.astype(F32)).astype(BF16)


def dot(left, right, left_dim, right_dim):
    left_high, left_low = halves(left)
    right_high, right_low = halves(right)
    small = contract(left_high, right_low, left_dim, right_dim) + contract(
        left_low, right_high, left_dim, right_dim
    )
    return contract(left_high, right_high, left_dim, right_dim) + small


def grid_index():
    row = lax.broadcasted_iota(jnp.int32, (BLOCK, BLOCK), 0)
    column = lax.broadcasted_iota(jnp.int32, (BLOCK, BLOCK), 1)
    return row, column


def to_row(column_vector):
    row, column = grid_index()
    return jnp.sum(jnp.where(row == column, column_vector, 0.0), 0, keepdims=True)


def to_column(row_vector):
    row, column = grid_index()
    return jnp.sum(jnp.where(row == column, row_vector, 0.0), 1, keepdims=True)


def unit_lower_inverses(lowers):
    row, column = grid_index()
    span = 1
    results = None
    while span < BLOCK:
        pair = (row // (2 * span) == column // (2 * span)) & (row // span != column // span)
        corners = [jnp.where(pair, lower, 0.0) for lower in lowers]
        if results is None:
            identity = (row == column).astype(F32)
            results = [identity - corner for corner in corners]
        else:
            halves = [dot(corner, result, 1, 0) for corner, result in zip(corners, results)]
            results = [result - dot(result, half, 1, 0) for result, half in zip(results, halves)]
        span = span * 2
    return results


def inverse_rms(rows, epsilon):
    return lax.rsqrt(jnp.mean(rows * rows, -1, keepdims=True) + epsilon)


def softplus(value):
    return jnp.maximum(value, 0.0) + jnp.log1p(jnp.exp(-jnp.abs(value)))


class Refs:
    def __init__(self, names, refs):
        for name, ref in zip(names, refs):
            setattr(self, name, ref)


Z_X, Z_COT, Z_WOUT, Z_DN2, Z_DRES, Z_Y, Z_DN1, Z_SMALL, Z_MIXED = range(9)


def kernel(cfg, names, *refs):
    r = Refs(names, refs)
    T, N, S, R, L, D = cfg["T"], cfg["N"], cfg["S"], cfg["R"], cfg["L"], cfg["D"]
    NI, F, HID, c0, c1, ca = (cfg[name] for name in ("NI", "F", "HID", "c0", "c1", "ca"))
    bits = N.bit_length() - 1
    blocks = L // BLOCK
    me_z = lax.axis_index("tensor")
    me_d = lax.axis_index("dp")
    sends = []

    def bit(b):
        return lax.rem(lax.div(me_d, 1 << b), 2)

    def flipped(which):
        place = me_d
        for b in which:
            place = place + (1 << b) * (1 - 2 * bit(b))
        return place

    barrier = pltpu.get_barrier_semaphore()
    for p in range(T):

        @pl.when(p != me_z)
        def _():
            pl.semaphore_signal(barrier, inc=1, device_id={"tensor": p}, device_id_type=MESH)

    for b in range(bits):
        pl.semaphore_signal(barrier, inc=1, device_id={"dp": flipped([b])}, device_id_type=MESH)

    far = T >= 3
    relays = ((0, 1, T - 2), (T - 1, T - 2, 1))

    def z_copy(k, device, src, dst, sent, received):
        return pltpu.make_async_remote_copy(
            src_ref=src,
            dst_ref=dst,
            send_sem=r.z_send.at[k, sent],
            recv_sem=r.z_recv.at[k, received],
            device_id={"tensor": device},
            device_id_type=MESH,
        )

    def z_start(condition, *copy):
        @pl.when(condition)
        def _():
            z_copy(*copy).start()

        sends.append((condition, copy))

    def z_take(condition, k, landing, received):
        @pl.when(condition)
        def _():
            z_copy(k, me_z, landing, landing, 0, received).wait_recv()

    def between(p):
        if far and p in (0, T - 1):
            return (me_z != 0) & (me_z != T - 1)
        return me_z != p

    def gather_start(k, place):
        def to(condition, p):
            z_start(condition, k, p, place(me_z), place(me_z), p, me_z)

        if far:
            to(me_z == 0, T - 2)
        for p in range(T):
            to(between(p) & (me_z != 0) if far and p == T - 2 else between(p), p)

    def gather_relay(k, place):
        if far:
            for n, (end, _, passing) in enumerate(relays):
                z_take(me_z == passing, k, place(end), end)
                z_start(me_z == passing, k, T - 1 - end, place(end), place(end), T + n, end)

    def gather_wait(k, place, then=None):
        for p in range(T):
            here = me_z != p
            for end, _, passing in relays if far else ():
                if end == p:
                    here = here & (me_z != passing)
            z_take(here, k, place(p), p)
            if then is not None:
                pl.when(me_z != p)(functools.partial(then, p))

    def rows_for(ref, p):
        return ref.at[pl.ds(p * R, R), :]

    def sum_start(k, send, recv, via, peers):
        for n, (end, near, _) in enumerate(relays if far else ()):
            p = T - 1 - end
            if p in peers:
                z_start(me_z == end, k, near, rows_for(send, p), via.at[n], p, T + n)
        for p in peers:
            direct = me_z != p
            for end, near, _ in relays if far else ():
                if p == T - 1 - end:
                    direct = direct & (me_z != end) & (me_z != near)
            z_start(direct, k, p, rows_for(send, p), recv.at[me_z], p, me_z)

    def sum_relay(k, send, recv, via):
        for n, (end, near, passing) in enumerate(relays if far else ()):
            p = T - 1 - end
            z_take(me_z == near, k, via.at[n], T + n)

            @pl.when(me_z == near)
            def _():
                rows = pl.ds(p * R, R)
                send[rows, :] = (send[rows, :].astype(F32) + via[n].astype(F32)).astype(BF16)

            z_start(me_z == near, k, p, rows_for(send, p), recv.at[near], p, near)

    def sum_clear(recv):
        for end, _, _ in relays if far else ():

            @pl.when(me_z == end)
            def _():
                recv[T - 1 - end] = jnp.zeros((R, D), BF16)

    def sum_wait(k, recv):
        for p in range(T):
            z_take(between(p), k, recv.at[p], p)

    class Gather:
        def __init__(self, index, place, order):
            self.index, self.place, self.order = index, place, order

        def copies(self, s, arriving):
            out = []
            for subset in range(1 << s):
                which = [self.order[t] for t in range(s) if subset >> t & 1]
                j = flipped(which + ([self.order[s]] if arriving else []))
                n = (1 << s) - 1 + subset
                out.append(
                    pltpu.make_async_remote_copy(
                        src_ref=self.place(j),
                        dst_ref=self.place(j),
                        send_sem=r.g_send.at[self.index, n],
                        recv_sem=r.g_recv.at[self.index, n],
                        device_id={"dp": flipped([self.order[s]])},
                        device_id_type=MESH,
                    )
                )
            return out

        def start(self, s):
            if s < bits:
                for copy in self.copies(s, False):
                    copy.start()

        def wait(self, s):
            if s < bits:
                for copy in self.copies(s, True):
                    copy.wait_recv()

        def step(self, s):
            self.wait(s)
            self.start(s + 1)

        def finish(self, s):
            for t in range(s, bits):
                self.step(t)

        def drain(self):
            for s in range(bits):
                for copy in self.copies(s, False):
                    copy.wait_send()

    upward = list(range(1, bits)) + [0]
    downward = list(reversed(range(1, bits))) + [0]

    def shard_of(ref, first=0, end=None):
        end = ref.shape[1] if end is None else end
        return lambda j: ref.at[pl.ds(pl.multiple_of(j * S, S), S), first:end]

    def shard_of3(ref):
        return lambda j: ref.at[:, pl.ds(pl.multiple_of(j * S, S), S), :]

    own_rows = pl.ds(pl.multiple_of(me_d * S, S), S)
    g_in = Gather(0, shard_of(r.w_in_all, 0, c0), upward)
    g_ig = Gather(4, shard_of(r.w_in_all, c0, NI), downward)
    g_gu = Gather(1, shard_of(r.w_gu_all), upward)
    g_d = Gather(2, shard_of(r.w_d_all), downward)
    g_out = Gather(3, shard_of3(r.w_out_all), upward)

    class Reduce:
        def __init__(self, index, keep, send, recv, out, order):
            self.index, self.keep, self.send, self.recv, self.out = index, keep, send, recv, out
            self.order = order

        def copy(self, level):
            return pltpu.make_async_remote_copy(
                src_ref=self.send[level],
                dst_ref=self.recv[level],
                send_sem=r.r_send.at[self.index, level],
                recv_sem=r.r_recv.at[self.index, level],
                device_id={"dp": flipped([self.order[level]])},
                device_id_type=MESH,
            )

        def start(self, level):
            self.copy(level).start()

        def step(self, level):
            self.copy(level).wait_recv()
            keep, recv = self.keep, self.recv[level]

            def part(j):
                rows = pl.ds(pl.multiple_of(j * S, S), S)
                return keep[rows, :] + recv[rows, :].astype(F32)

            if level + 1 == bits:
                self.out[...] = part(0)
                return
            half = N >> (level + 2)
            mine = bit(self.order[level + 1])
            low_first = self.order is reduce_up

            def body(q, carry):
                if low_first:
                    a, b = 2 * q + mine, 2 * q + 1 - mine
                else:
                    a, b = q + half * mine, q + half * (1 - mine)
                stay, leave = part(a), part(b)
                rows = pl.ds(pl.multiple_of(q * S, S), S)
                keep[rows, :] = stay
                self.send[level + 1][rows, :] = leave.astype(BF16)
                return carry

            lax.fori_loop(0, half, body, 0)
            self.start(level + 1)

        def drain(self):
            for level in range(bits):
                self.copy(level).wait_send()

    reduce_up = [0] + list(range(1, bits))
    reduce_down = [0] + list(reversed(range(1, bits)))

    def levels(prefix):
        return [getattr(r, prefix + str(level)) for level in range(bits)]

    s_a = Reduce(0, r.k_a, levels("s_a"), levels("v_a"), r.o_a, reduce_up)
    s_b = Reduce(4, r.k_b, levels("s_b"), levels("v_b"), r.o_b, reduce_down)
    s_og = Reduce(5, r.k_og, levels("s_og"), levels("v_og"), r.o_og, reduce_down)
    s_gu = Reduce(1, r.k_gu, levels("s_gu"), levels("v_gu"), r.o_gu, reduce_up)
    s_d = Reduce(2, r.k_d, levels("s_d"), levels("v_d"), r.o_d, reduce_down)
    s_out = Reduce(3, r.k_out, levels("s_out"), levels("v_out"), r.o_out, reduce_down)

    def transpose_into(source):
        for i in range(blocks):
            here = slice(i * BLOCK, (i + 1) * BLOCK)
            r.turned[:, here] = source[here, :].T

    def weight_grad(right, columns, sum_of, at):
        wide = columns.stop - columns.start

        def body(p, carry):
            pair = pl.ds(pl.multiple_of(p * 2 * S, 2 * S), 2 * S)
            rows = pl.ds(pl.multiple_of(p * S, S), S)
            r.pair[:, :wide] = nn(r.turned[pair, :], right[:, columns])
            mine, other = bit(0) * S, (1 - bit(0)) * S
            sum_of.keep[rows, at : at + wide] = r.pair[pl.ds(pl.multiple_of(mine, S), S), :wide]
            sum_of.send[0][rows, at : at + wide] = r.pair[
                pl.ds(pl.multiple_of(other, S), S), :wide
            ].astype(BF16)
            return carry

        lax.fori_loop(0, N // 2, body, 0)

    def block_rows(p):
        return pl.ds(p * R if isinstance(p, int) else pl.multiple_of(p * R, R), R)

    own = block_rows(me_z)

    def rows_place(ref):
        return lambda p: ref.at[block_rows(p), :]

    r.x_all[own, :] = r.x[...]
    r.w_in_all[own_rows, :c0] = r.w_qkv[...]
    r.w_in_all[own_rows, c0:c1] = r.w_og[...]
    place = lax.broadcasted_iota(jnp.int32, (LANES, S), 0)
    both = jnp.where(place == 0, r.w_beta[...].astype(F32), 0.0)
    both = jnp.where(place == 1, r.w_alpha[...].astype(F32), both)
    r.w_in_all[own_rows, c1:] = both.T.astype(BF16)
    pl.semaphore_wait(barrier, T - 1 + bits)
    gather_start(Z_X, rows_place(r.x_all))
    g_in.start(0)
    g_ig.start(0)
    r.w_d_all[own_rows, :] = jnp.zeros((S, F), BF16)
    r.w_gu_all[own_rows, :] = jnp.zeros((S, 2 * F), BF16)
    r.w_d_all[own_rows, :HID] = r.w_down[...].T
    r.w_out_all[me_z, own_rows, :] = r.w_out[...].T
    r.w_gu_all[own_rows, :HID] = r.w_gate[...].T
    r.w_gu_all[own_rows, F : F + HID] = r.w_up[...].T
    r.cot_all[own, :] = r.cot[...]
    for recv in (r.dn2_recv, r.y_recv, r.dn1_recv):
        sum_clear(recv)

    def first_norm(rows):
        x = r.x_all[rows, :].astype(F32)
        r.n1[rows, :] = (x * inverse_rms(x, 1e-06) * r.gain1[...]).astype(BF16)

    g_ig.step(0)
    g_in.step(0)
    first_norm(own)
    segment = r.seg[...].astype(F32)
    r.segc[0:PAD, :] = jnp.full((PAD, 1), -1.0, F32)
    r.segc[PAD + L :, :] = jnp.full((PAD, 1), -2.0, F32)
    for i in range(blocks):
        r.segc[PAD + i * BLOCK : PAD + (i + 1) * BLOCK, :] = to_column(
            segment[:, i * BLOCK : (i + 1) * BLOCK]
        )
    r.proj[0:PAD, :] = jnp.zeros((PAD, NI), F32)
    r.dtot[L:, :] = jnp.zeros((PAD, c0), F32)
    g_ig.step(1)
    g_in.step(1)
    g_d.start(0)
    g_gu.start(0)

    def out_place(p):
        return r.w_out_all.at[p, own_rows, :]

    gather_relay(Z_X, rows_place(r.x_all))
    gather_wait(Z_X, rows_place(r.x_all))
    gather_start(Z_WOUT, out_place)
    gather_start(Z_COT, rows_place(r.cot_all))
    for p in range(T):
        pl.when(me_z != p)(functools.partial(first_norm, block_rows(p)))
    g_ig.finish(2)
    g_in.finish(2)
    g_d.step(0)
    g_gu.step(0)
    chunk = 2 * R
    chunks = [slice(i * chunk, (i + 1) * chunk) for i in range(L // chunk)]
    for c in chunks:
        r.proj[PAD + c.start : PAD + c.stop, :] = nn(r.n1[c, :], r.w_in_all[...])
    gather_relay(Z_WOUT, out_place)
    row, column = grid_index()
    inclusive = row >= column

    def shifted_segment(i, o):
        return r.segc[PAD + i * BLOCK + o : PAD + (i + 1) * BLOCK + o, :]

    def conv_total(i):
        base = PAD + i * BLOCK
        now = shifted_segment(i, 0)
        total = r.conv_w[3:4, :] * r.proj[base : base + BLOCK, :c0]
        for o in range(1, 4):
            same = (shifted_segment(i, -o) == now).astype(F32)
            total = total + r.conv_w[3 - o : 4 - o, :] * (
                r.proj[base - o : base - o + BLOCK, :c0] * same
            )
        return total

    def decays(i):
        base = PAD + i * BLOCK
        both = r.proj[base : base + BLOCK, c1:]
        beta = jax.nn.sigmoid(both[:, 0:1])
        before = both[:, 1:2] + r.dt_bias[...]
        log_decay = -jnp.exp(r.a_log[...]) * softplus(before)
        cum_row = jnp.sum(jnp.where(row <= column, log_decay, 0.0), 0, keepdims=True)
        cum = to_column(cum_row)
        seg_col = shifted_segment(i, 0)
        seg_row = segment[:, i * BLOCK : (i + 1) * BLOCK]
        keep = (seg_col == seg_row) & inclusive
        ratio = jnp.where(keep, jnp.exp(jnp.where(keep, cum - cum_row, 0.0)), 0.0)
        first = PAD + i * BLOCK
        carry = jnp.where(seg_col == r.segc[first - 1 : first, :], jnp.exp(cum), 0.0)
        ends = to_column(ratio[BLOCK - 1 : BLOCK, :])
        last = carry[BLOCK - 1 : BLOCK, :]
        return beta, before, log_decay, ratio, carry, ends, last

    def rows_of(i):
        return slice(i * BLOCK, (i + 1) * BLOCK)

    def mixed_place(i):
        return lambda p: r.mixed_all.at[p, pl.ds(i * BLOCK, BLOCK), :]

    lowers = []
    for i in range(blocks):
        here = rows_of(i)
        total = conv_total(i)
        active = total * jax.nn.sigmoid(total)
        q, k, v = active[:, :DK], active[:, DK : 2 * DK], active[:, 2 * DK :]
        q = q * lax.rsqrt(jnp.sum(q * q, -1, keepdims=True) + 1e-06) * DK ** (-0.5)
        k = k * lax.rsqrt(jnp.sum(k * k, -1, keepdims=True) + 1e-06)
        r.q[here, :], r.k[here, :], r.v[here, :] = q, k, v
        beta, _, _, ratio, carry, ends, last = decays(i)
        r.ratio[here, :] = ratio
        lowers.append(jnp.where(row > column, beta * ratio * dot(k, k, 1, 1), 0.0))
        if i == 1:
            gather_wait(Z_WOUT, out_place)
            g_out.start(0)
    g_d.step(1)
    inverse_list = unit_lower_inverses(lowers)
    for i in range(blocks):
        r.inverses[rows_of(i), :] = inverse_list[i]
    state = jnp.zeros((DV, DK), F32)
    for i in range(blocks):
        here = rows_of(i)
        r.states[i * DV : (i + 1) * DV, :] = state
        beta, _, _, ratio, carry, ends, last = decays(i)
        keys, query = r.k[here, :], r.q[here, :]
        target = beta * (r.v[here, :] - carry * dot(keys, state, 1, 1))
        update = dot(r.inverses[here, :], target, 1, 0)
        r.u[here, :] = update
        weights = ratio * dot(query, keys, 1, 1)
        o = carry * dot(query, state, 1, 1) + dot(weights, update, 1, 0)
        r.o[here, :] = o
        state = last * state + dot(update * ends, keys, 0, 0)
        gate = r.proj[PAD + here.start : PAD + here.stop, c0:c1]
        mixed = o * inverse_rms(o, 1e-05) * r.out_gain[...] * (gate * jax.nn.sigmoid(gate))
        r.mixed_all[me_z, here, :] = mixed.astype(BF16)
        gather_start(Z_MIXED + i, mixed_place(i))
    gather_relay(Z_COT, rows_place(r.cot_all))
    g_out.step(0)
    g_gu.step(1)
    g_d.finish(2)
    for i in range(chunk // BLOCK):
        gather_relay(Z_MIXED + i, mixed_place(i))
    g_out.step(1)
    g_gu.finish(2)
    g_out.finish(2)
    gather_wait(Z_COT, rows_place(r.cot_all))

    ffn_gain_sum = jnp.zeros((1, D), F32)
    for c in chunks:
        of_chunk = range(c.start // BLOCK, c.stop // BLOCK)
        for i in of_chunk:
            gather_wait(Z_MIXED + i, mixed_place(i))
        total = r.x_all[c, :].astype(F32)
        for h in range(T):
            total = total + nt(r.mixed_all[h, c, :], r.w_out_all[h])
        r.resid[c, :] = total
        hhat = total * inverse_rms(total, 1e-06)
        r.n2[c, :] = (hhat * r.gain2[...]).astype(BF16)
        fgate = nn(r.n2[c, :], r.w_gu_all[:, :F])
        fup = nn(r.n2[c, :], r.w_gu_all[:, F:])
        for i in range(c.stop // BLOCK, blocks) if c.start == 0 else ():
            gather_relay(Z_MIXED + i, mixed_place(i))
        dhidden = nn(r.cot_all[c, :], r.w_d_all[...])
        sigma = jax.nn.sigmoid(fgate)
        gated = fgate * sigma
        r.hidden[c, :] = (gated * fup).astype(BF16)
        r.dgu[c, F:] = (dhidden * gated).astype(BF16)
        r.dgu[c, :F] = (dhidden * fup * sigma * (1.0 + fgate * (1.0 - sigma))).astype(BF16)
        dn2 = nt(r.dgu[c, :], r.w_gu_all[...])
        r.dn2_send[c, :] = dn2.astype(BF16)
        sum_start(Z_DN2, r.dn2_send, r.dn2_recv, r.dn2_via, range(c.start // R, c.stop // R))
        total = r.resid[c, :]
        hhat = total * inverse_rms(total, 1e-06)
        ffn_gain_sum = ffn_gain_sum + jnp.sum(dn2 * hhat, 0, keepdims=True)
    r.small_z[me_z] = jnp.zeros((8, D), F32)
    r.small_z[me_z, 1:2, :] = ffn_gain_sum
    transpose_into(r.cot_all)
    weight_grad(r.hidden, slice(0, F), s_d, 0)
    s_d.start(0)
    sum_relay(Z_DN2, r.dn2_send, r.dn2_recv, r.dn2_via)
    transpose_into(r.n2)
    weight_grad(r.dgu, slice(0, F), s_gu, 0)
    weight_grad(r.dgu, slice(F, 2 * F), s_gu, F)
    s_gu.start(0)
    s_d.step(0)
    for c in chunks:
        r.y_send[c, :] = nt(r.hidden[c, :], r.w_d_all[...]).astype(BF16)
    s_gu.step(0)
    sum_wait(Z_DN2, r.dn2_recv)

    def summed(own_send, received):
        total = own_send[own, :].astype(F32)
        for d in range(1, T):
            total = total + received[lax.rem(me_z + d, T)].astype(F32)
        return total

    def norm_back(total, gain, upstream):
        inverse = inverse_rms(total, 1e-06)
        hat = total * inverse
        e = upstream * gain
        return inverse * (e - hat * jnp.mean(e * hat, -1, keepdims=True))

    dresid = r.cot[...].astype(F32) + norm_back(
        r.resid[own, :], r.gain2[...], summed(r.dn2_send, r.dn2_recv)
    )
    r.dresid[...] = dresid
    r.dres_all[own, :] = dresid.astype(BF16)
    gather_start(Z_DRES, rows_place(r.dres_all))
    s_d.step(1)
    gather_relay(Z_DRES, rows_place(r.dres_all))
    gather_wait(Z_DRES, rows_place(r.dres_all))
    sum_start(Z_Y, r.y_send, r.y_recv, r.y_via, range(T))
    transpose_into(r.dres_all)
    weight_grad(r.mixed_all.at[me_z], slice(0, DV), s_out, 0)
    s_out.start(0)

    out_gain_sum = jnp.zeros((1, DV), F32)
    for i in range(blocks):
        here = rows_of(i)
        base = PAD + i * BLOCK
        dmixed = nn(r.dres_all[here, :], r.w_out_all[me_z])
        gate = r.proj[base : base + BLOCK, c0:c1]
        o = r.o[here, :]
        inverse = inverse_rms(o, 1e-05)
        o_hat = o * inverse
        sg = jax.nn.sigmoid(gate)
        dgate = dmixed * (o_hat * r.out_gain[...]) * sg * (1.0 + gate * (1.0 - sg))
        r.dproj[here, c0:c1] = dgate.astype(BF16)
        dnormed = dmixed * (gate * sg)
        out_gain_sum = out_gain_sum + jnp.sum(dnormed * o_hat, 0, keepdims=True)
        e = dnormed * r.out_gain[...]
        r.o[here, :] = inverse * (e - o_hat * jnp.mean(e * o_hat, -1, keepdims=True))
    s_out.step(0)
    transpose_into(r.n1)
    weight_grad(r.dproj, slice(c0, c1), s_og, 0)
    s_og.start(0)
    lane = lax.broadcasted_iota(jnp.int32, (1, LANES), 1)
    dstate = jnp.zeros((DV, DK), F32)
    conv_sums = [jnp.zeros((1, c0), F32) for _ in range(4)]
    a_log_sum = jnp.zeros((1, 1), F32)
    dt_sum = jnp.zeros((1, 1), F32)
    for i in reversed(range(blocks)):
        here = rows_of(i)
        base = PAD + i * BLOCK
        grad = r.o[here, :]
        state = r.states[i * DV : (i + 1) * DV, :]
        beta, before, log_decay, scale, carried, ends, last = decays(i)
        keys, query, update = r.k[here, :], r.q[here, :], r.u[here, :]
        kk = dot(keys, keys, 1, 1)
        qk = dot(query, keys, 1, 1)
        key_state = dot(keys, state, 1, 1)
        query_state = dot(query, state, 1, 1)
        rest = r.v[here, :] - carried * key_state
        key_dstate = dot(keys, dstate, 1, 1)
        dupdate = dot(scale * qk, grad, 0, 0) + ends * key_dstate
        dends = jnp.sum(key_dstate * update, -1, keepdims=True)
        dweights = dot(grad, update, 1, 1)
        dqk = dweights * scale
        dtarget = dot(r.inverses[here, :], dupdate, 0, 0)
        dlower = jnp.where(row > column, -dot(dtarget, update, 1, 1), 0.0)
        lower_kk = dlower * kk
        dbeta = jnp.sum(dtarget * rest, -1, keepdims=True) + jnp.sum(
            lower_kk * scale, -1, keepdims=True
        )
        drest = beta * dtarget
        dv = drest
        dcarry = jnp.sum(grad * query_state - drest * key_state, -1, keepdims=True)
        dratio = dweights * qk + beta * lower_kk
        dkk = dlower * beta * scale
        dquery_state = carried * grad
        dkey_state = -carried * drest
        dq = dot(dquery_state, state, 1, 0) + dot(dqk, keys, 1, 0)
        dk = (
            dot(update * ends, dstate, 1, 0)
            + dot(dqk, query, 0, 0)
            + dot(dkey_state, state, 1, 0)
            + dot(dkk, keys, 1, 0)
            + dot(dkk, keys, 0, 0)
        )
        dlast = jnp.sum(jnp.sum(dstate * state, 0, keepdims=True), 1, keepdims=True)
        dstate = (
            last * dstate + dot(dquery_state, query, 0, 0) + dot(dkey_state, keys, 0, 0)
        )

        weight = dratio * scale
        ended = dends * ends
        at_last = (lax.broadcasted_iota(jnp.int32, (BLOCK, 1), 0) == BLOCK - 1).astype(F32)
        dcum = (
            jnp.sum(weight, 1, keepdims=True)
            - to_column(jnp.sum(weight, 0, keepdims=True))
            - ended
            + dcarry * carried
            + at_last * (jnp.sum(ended, 0, keepdims=True) + dlast * last)
        )
        dlog = jnp.sum(jnp.where(column >= row, to_row(dcum), 0.0), 1, keepdims=True)
        a_log_sum = a_log_sum + jnp.sum(dlog * log_decay, 0, keepdims=True)
        ddecay = dlog * -jnp.exp(r.a_log[...]) * jax.nn.sigmoid(before)
        dt_sum = dt_sum + jnp.sum(ddecay, 0, keepdims=True)
        dbeta_in = dbeta * beta * (1.0 - beta)
        r.dproj[here, c1:] = jnp.where(
            lane == 0, dbeta_in, jnp.where(lane == 1, ddecay, 0.0)
        ).astype(BF16)

        total = conv_total(i)
        st = jax.nn.sigmoid(total)
        active = total * st
        slope = st * (1.0 + total * (1.0 - st))
        q, k = active[:, :DK], active[:, DK : 2 * DK]
        rq = lax.rsqrt(jnp.sum(q * q, -1, keepdims=True) + 1e-06)
        rk = lax.rsqrt(jnp.sum(k * k, -1, keepdims=True) + 1e-06)
        dq = dq * DK ** (-0.5)
        dq = rq * (dq - q * (rq * rq * jnp.sum(dq * q, -1, keepdims=True)))
        dk = rk * (dk - k * (rk * rk * jnp.sum(dk * k, -1, keepdims=True)))
        r.dtot[here, :DK] = dq * slope[:, :DK]
        r.dtot[here, DK : 2 * DK] = dk * slope[:, DK : 2 * DK]
        r.dtot[here, 2 * DK :] = dv * slope[:, 2 * DK :]
        dtotal = r.dtot[here, :]
        now = shifted_segment(i, 0)
        conv_sums[3] = conv_sums[3] + jnp.sum(
            dtotal * r.proj[base : base + BLOCK, :c0], 0, keepdims=True
        )
        dmixer = r.conv_w[3:4, :] * dtotal
        for o_ in range(1, 4):
            same = (shifted_segment(i, -o_) == now).astype(F32)
            conv_sums[3 - o_] = conv_sums[3 - o_] + jnp.sum(
                dtotal * same * r.proj[base - o_ : base - o_ + BLOCK, :c0], 0, keepdims=True
            )
            later = (shifted_segment(i, o_) == now).astype(F32)
            dmixer = dmixer + r.conv_w[3 - o_ : 4 - o_, :] * (
                later * r.dtot[i * BLOCK + o_ : (i + 1) * BLOCK + o_, :]
            )
        r.dproj[here, :c0] = dmixer.astype(BF16)
        if i == blocks - 1:
            s_og.step(0)
            s_out.step(1)
        if i == blocks - 2:
            s_gu.step(1)
            s_d.step(2)
        if i == blocks - 3:
            s_og.step(1)
            s_out.step(2)
    sum_relay(Z_Y, r.y_send, r.y_recv, r.y_via)

    attn_gain_sum = jnp.zeros((1, D), F32)
    for c in chunks:
        dn1 = nt(r.dproj[c, :], r.w_in_all[...])
        r.n2[c, :] = dn1.astype(BF16)
        x = r.x_all[c, :].astype(F32)
        attn_gain_sum = attn_gain_sum + jnp.sum(dn1 * (x * inverse_rms(x, 1e-06)), 0, keepdims=True)
    r.small_z[me_z, 0:1, :] = attn_gain_sum
    r.small_z[me_z, 2:3, :DV] = out_gain_sum
    for t in range(4):
        r.small_z[me_z, 3 + t : 4 + t, :c0] = conv_sums[t]
    r.small_z[me_z, 7:8, :LANES] = jnp.where(lane == 0, a_log_sum, jnp.where(lane == 1, dt_sum, 0.0))
    for p in range(T):
        z_start(me_z != p, Z_SMALL, p, r.small_z.at[me_z], r.small_z.at[me_z], p, me_z)
    sum_start(Z_DN1, r.n2, r.dn1_recv, r.dn1_via, range(T))
    weight_grad(r.dproj, slice(0, ca), s_a, 0)
    s_a.start(0)
    weight_grad(r.dproj, slice(ca, c0), s_b, 0)
    weight_grad(r.dproj, slice(c1, NI), s_b, c0 - ca)
    s_b.start(0)
    s_a.step(0)
    s_b.step(0)
    for p in range(T):
        z_take(me_z != p, Z_SMALL, r.small_z.at[p], p)
    everywhere = r.small_z[0]
    for p in range(1, T):
        everywhere = everywhere + r.small_z[p]
    which = lax.broadcasted_iota(jnp.int32, (8, D), 0)
    small = jnp.where(which < 3, everywhere, r.small_z[me_z])

    def small_copy(level):
        return pltpu.make_async_remote_copy(
            src_ref=r.small_s.at[level],
            dst_ref=r.small_v.at[level],
            send_sem=r.a_send.at[level],
            recv_sem=r.a_recv.at[level],
            device_id={"dp": flipped([level])},
            device_id_type=MESH,
        )

    def small_start(level, value):
        r.small_s[level] = value
        small_copy(level).start()

    def small_step(level):
        small_copy(level).wait_recv()
        return r.small_s[level] + r.small_v[level]

    small_start(0, small)
    sum_relay(Z_DN1, r.n2, r.dn1_recv, r.dn1_via)
    for level in range(2, bits):
        s_gu.step(level)
        s_og.step(level)
        if level > 2:
            s_d.step(level)
            s_out.step(level)
    for level in range(bits):
        small = small_step(level)
        if level + 1 < bits:
            small_start(level + 1, small)
        if level > 0:
            s_b.step(level)
            s_a.step(level)
    sum_wait(Z_Y, r.y_recv)
    r.o_block[...] = (r.resid[own, :] + summed(r.y_send, r.y_recv)).astype(BF16)
    r.o_small[...] = small
    sum_wait(Z_DN1, r.dn1_recv)
    r.o_input[...] = r.dresid[...] + norm_back(
        r.x[...].astype(F32), r.gain1[...], summed(r.n2, r.dn1_recv)
    )

    for condition, copy in sends:

        @pl.when(condition)
        def _():
            z_copy(*copy).wait_send()

    for gather in (g_in, g_ig, g_gu, g_d, g_out):
        gather.drain()
    for reduce in (s_a, s_b, s_og, s_gu, s_d, s_out):
        reduce.drain()
    for level in range(bits):
        small_copy(level).wait_send()


def unpack(cfg, parts, *refs):
    count = len(parts)
    given, outs, here, sems = refs[:count], refs[count:-count - 1], refs[-count - 1 : -1], refs[-1]
    (block, inputs, attn, qkv, og, beta, alpha, conv, a_log, dt, gain, out, ffn, gate, up, down) = outs
    c0, ca, HID, F = cfg["c0"], cfg["ca"], cfg["HID"], cfg["F"]
    copies = [
        pltpu.make_async_copy(source, place, sems.at[n])
        for n, (source, place) in enumerate(zip(given, here))
    ]
    for copy in copies:
        copy.start()
    g = Refs(["h" + part[1:] for part in parts], here)
    arrived = dict(zip(parts, copies))
    arrived["o_gu"].wait()
    gate[...] = g.h_gu[:, :F].T[:HID, :]
    up[...] = g.h_gu[:, F:].T[:HID, :]
    arrived["o_d"].wait()
    down[...] = g.h_d[...].T[:HID, :]
    arrived["o_a"].wait()
    qkv[:, :ca] = g.h_a[...]
    arrived["o_b"].wait()
    qkv[:, ca:] = g.h_b[:, : c0 - ca]
    both = g.h_b[:, c0 - ca :].T
    beta[...] = both[0:1, :]
    alpha[...] = both[1:2, :]
    arrived["o_og"].wait()
    og[...] = g.h_og[...]
    arrived["o_small"].wait()
    attn[...] = g.h_small[0:1, :]
    ffn[...] = g.h_small[1:2, :]
    gain[...] = g.h_small[2:3, : gain.shape[1]]
    conv[...] = g.h_small[3:7, :c0]
    a_log[...] = g.h_small[7:8, 0:1]
    dt[...] = g.h_small[7:8, 1:2]
    arrived["o_out"].wait()
    out[...] = g.h_out[...].T
    arrived["o_block"].wait()
    block[...] = g.h_block[...]
    arrived["o_input"].wait()
    inputs[...] = g.h_input[...]


def fused(T, N, c0, c1, args):
    R, D = args["x"].shape
    S = args["w_qkv"].shape[0]
    NI = c1 + LANES
    HID = args["w_down"].shape[0]
    F = HID + -HID % LANES
    L = args["seg"].shape[1]
    ca = c0 - LANES
    wides = {"a": ca, "b": NI - ca - (c1 - c0), "og": c1 - c0, "gu": 2 * F, "d": F, "out": DV}
    bits = N.bit_length() - 1
    blocks = L // BLOCK
    outs = {
        "o_block": ((R, D), BF16),
        "o_input": ((R, D), F32),
        **{"o_" + name: ((S, wide), F32) for name, wide in wides.items()},
        "o_small": ((8, D), F32),
    }
    scratch = {
        "x_all": ((L, D), BF16),
        "cot_all": ((L, D), BF16),
        "w_in_all": ((D, NI), BF16),
        "w_gu_all": ((D, 2 * F), BF16),
        "w_d_all": ((D, F), BF16),
        "w_out_all": ((T, D, DV), BF16),
        "n1": ((L, D), BF16),
        "n2": ((L, D), BF16),
        "proj": ((PAD + L, NI), F32),
        "segc": ((PAD + L + PAD, 1), F32),
        "q": ((L, DK), F32),
        "k": ((L, DK), F32),
        "v": ((L, DV), F32),
        "ratio": ((L, BLOCK), F32),
        "inverses": ((L, BLOCK), F32),
        "states": ((blocks * DV, DK), F32),
        "u": ((L, DV), F32),
        "o": ((L, DV), F32),
        "mixed_all": ((T, L, DV), BF16),
        "resid": ((L, D), F32),
        "hidden": ((L, F), BF16),
        "dgu": ((L, 2 * F), BF16),
        "dn2_send": ((L, D), BF16),
        "dn2_recv": ((T, R, D), BF16),
        "dn2_via": ((2, R, D), BF16),
        "y_send": ((L, D), BF16),
        "y_recv": ((T, R, D), BF16),
        "y_via": ((2, R, D), BF16),
        "dn1_recv": ((T, R, D), BF16),
        "dn1_via": ((2, R, D), BF16),
        "dresid": ((R, D), F32),
        "dres_all": ((L, D), BF16),
        "dtot": ((L + PAD, c0), F32),
        "dproj": ((L, NI), BF16),
        "turned": ((D, L), BF16),
        "pair": ((2 * S, max(F, ca)), F32),
        "small_z": ((T, 8, D), F32),
        "small_s": ((bits, 8, D), F32),
        "small_v": ((bits, 8, D), F32),
    }
    for name, wide in wides.items():
        scratch["k_" + name] = ((N // 2 * S, wide), F32)
        for level in range(bits):
            rows = (N >> (level + 1)) * S
            scratch["s_" + name + str(level)] = ((rows, wide), BF16)
            scratch["v_" + name + str(level)] = ((rows, wide), BF16)
    semaphores = {
        "z_send": (Z_MIXED + blocks, T + 2),
        "z_recv": (Z_MIXED + blocks, T + 2),
        "g_send": (5, N - 1),
        "g_recv": (5, N - 1),
        "r_send": (6, bits),
        "r_recv": (6, bits),
        "a_send": (bits,),
        "a_recv": (bits,),
    }
    names = list(args) + list(outs) + list(scratch) + list(semaphores)
    cfg = {"T": T, "N": N, "S": S, "R": R, "L": L, "D": D, "NI": NI, "F": F}
    cfg.update({"HID": HID, "c0": c0, "c1": c1, "ca": ca})
    vmem = pl.BlockSpec(memory_space=pltpu.VMEM)
    result = pl.pallas_call(
        functools.partial(kernel, cfg, names),
        out_shape=[jax.ShapeDtypeStruct(*leaf) for leaf in outs.values()],
        in_specs=[vmem] * len(args),
        out_specs=[vmem] * len(outs),
        scratch_shapes=[pltpu.VMEM(*leaf) for leaf in scratch.values()]
        + [pltpu.SemaphoreType.DMA(shape) for shape in semaphores.values()],
        compiler_params=pltpu.CompilerParams(
            collective_id=0, has_side_effects=True, vmem_limit_bytes=63 * 2**20
        ),
    )(*args.values())
    got = dict(zip(outs, result))
    final = (
        ((R, D), BF16), ((R, D), F32), ((1, D), F32), ((S, c0), F32), ((S, c1 - c0), F32),
        ((1, S), F32), ((1, S), F32), (args["conv_w"].shape, F32), ((1, 1), F32), ((1, 1), F32),
        (args["out_gain"].shape, F32), ((DV, S), F32), ((1, D), F32), ((HID, S), F32),
        ((HID, S), F32), ((HID, S), F32),
    )
    parts = ("o_gu", "o_d", "o_a", "o_b", "o_og", "o_small", "o_out", "o_block", "o_input")
    return pl.pallas_call(
        functools.partial(unpack, cfg, parts),
        out_shape=[jax.ShapeDtypeStruct(*leaf) for leaf in final],
        in_specs=[pl.BlockSpec(memory_space=pl.ANY)] * len(parts),
        out_specs=[vmem] * len(final),
        scratch_shapes=[pltpu.VMEM(*outs[part]) for part in parts]
        + [pltpu.SemaphoreType.DMA((len(parts),))],
        compiler_params=pltpu.CompilerParams(vmem_limit_bytes=62 * 2**20),
    )(*[got[part] for part in parts])


def local(
    block_input,
    segment_ids,
    attention_norm_gain,
    w_qkv,
    w_og,
    w_beta,
    w_alpha,
    conv_weight,
    a_log,
    dt_bias,
    out_gain,
    w_out,
    ffn_gain,
    w_ffn_gate,
    w_ffn_up,
    w_ffn_down,
    cotangent,
):
    T, N = lax.axis_size("tensor"), lax.axis_size("dp")
    c0 = w_qkv.shape[1]
    c1 = c0 + w_og.shape[1]
    args = {
        "x": block_input,
        "seg": segment_ids,
        "gain1": attention_norm_gain[None],
        "w_qkv": w_qkv,
        "w_og": w_og,
        "w_beta": w_beta.T,
        "w_alpha": w_alpha.T,
        "w_gate": w_ffn_gate.T,
        "w_up": w_ffn_up.T,
        "w_down": w_ffn_down,
        "w_out": w_out,
        "conv_w": conv_weight,
        "a_log": a_log[None],
        "dt_bias": dt_bias[None],
        "out_gain": out_gain[None],
        "gain2": ffn_gain[None],
        "cot": cotangent,
    }
    (block, inputs, attn, qkv, og, beta, alpha, conv, a_log, dt, gain, out, ffn, gate, up, down) = fused(
        T, N, c0, c1, args
    )
    return (
        block, inputs, attn[0], qkv, og, beta.T, alpha.T, conv, a_log[0], dt[0], gain[0], out,
        ffn[0], gate.T, up.T, down,
    )


def solution(mesh):
    rows = P(("dp", "tensor"), None)
    split = P("dp", "tensor")
    turned = P("tensor", "dp")
    placed = (
        rows, P("dp", None), P(), split, split, split, split, P(None, "tensor"), P("tensor"),
        P("tensor"), P(), turned, P(), split, split, turned, rows,
    )
    given = (
        rows, rows, P(), split, split, split, split, P(None, "tensor"), P("tensor"), P("tensor"),
        P(), turned, P(), split, split, turned,
    )
    return jax.shard_map(local, mesh=mesh, in_specs=placed, out_specs=given, check_vma=False)
```
